128 devices in a mesh: leaf: 16 (over x, y), near: 8 (over z, core).
Axes of the slice: x: 4, y: 4, z: 4, core: 2. Of those that a mesh axis runs over, the one named last changes fastest.
Arguments:
- near_blocks: bfloat16 [512, 8, 256, 256], P(('leaf', 'near')), may hold values from -0.125 to 0.125
- near_index: int32 [512, 8], P(('leaf', 'near')), may hold values from 0 to 511, as said below
- test_vectors: bfloat16 [512, 64, 256], P(('leaf', 'near')), may hold values from -6 to 6
- samples: bfloat16 [512, 64, 256], P(('leaf', 'near')), may hold values from -6 to 6
- leaf_basis: bfloat16 [512, 64, 256], P(('leaf', 'near')), may hold values from -0.375 to 0.375
- col_weights: bfloat16 [512, 64, 64], P(('leaf', 'near')), may hold values from -0.75 to 0.75
- coupling: bfloat16 [512, 64, 2048], P(('leaf', 'near')), may hold values from -6 to 6
- adm_index: int32 [512, 32], P(('leaf', 'near')), may hold values from 0 to 511, as said below
- adm_count: int32 [512], P(('leaf', 'near')), may hold values from 2 to 32, as said below
- leaf_transfer: bfloat16 [512, 64, 64], P(('leaf', 'near')), may hold values from -0.75 to 0.75
- inner_transfer: bfloat16 [128, 3, 64, 64], P(('leaf', 'near')), may hold values from -0.75 to 0.75
- upper_transfer: bfloat16 [126, 64, 64], replicated, may hold values from -0.75 to 0.75
Outputs:
- leaf_factors: float32 [512, 64, 64], P(('leaf', 'near'))
- inner_factors: float32 [128, 3, 64, 64], P(('leaf', 'near'))
- upper_factors: float32 [128, 7, 64, 64], P(('leaf', 'near'))
The draws below stay inside these ranges and needn't reach their ends.
Inputs may be any that keep to these rules, and one draw needn't show every extreme that they name: `near_index`: leaves are the cells of a 3-D grid in Morton order: bit b of a leaf's number is bit b // 3 of its coordinate along dimension b mod 3. Entry 0 of each row is the row's own leaf; every entry is the leaf of a cell at most one step from the row's cell along each dimension. `adm_index`: with the leaves in the grid of near_index: slot 0 is the cell three steps back along every dimension and slot 1 three steps ahead, each coordinate clipped to the grid; slot 2 is the leaf whose number is the row's own with its highest bit flipped (the cell half the grid away along that bit's dimension); every other entry is the leaf of a cell at most three steps from the row's cell along each dimension. `adm_count`: in every aligned block of 4 leaves some leaf has 32 live slots.
All inputs are finite; a program needn't handle non-finite values.
Results may differ from the reference program's by a relative error of at most 0.0019.
Values may be sent and summed in bfloat16 or wider, within the bound.
No kernel may reach another device: no remote copies, remote signals or barrier semaphores. Data moves between devices by JAX's collectives and lax.ppermute only.
A program may use at most 128 MiB of HBM per device.

```python
import jax
import jax.numpy as jnp
from jax import lax

LEAF = 256
RANK = 64
NPD = 4
K = 8
MAXC = 32
LEAVES = 512
UP = 7
DEVICES = 128


def grid_coords(leaf_ids):
    total_bits = LEAVES.bit_length() - 1
    coords = [jnp.zeros_like(leaf_ids), jnp.zeros_like(leaf_ids), jnp.zeros_like(leaf_ids)]
    extents = [1, 1, 1]
    for bit in range(total_bits):
        coords[bit % 3] = coords[bit % 3] + ((leaf_ids >> bit & 1) << bit // 3)
        extents[bit % 3] = extents[bit % 3] * 2
    return (coords, extents)


def grid_ids(coords):
    total_bits = LEAVES.bit_length() - 1
    leaf_ids = jnp.zeros_like(coords[0])
    for bit in range(total_bits):
        leaf_ids = leaf_ids + ((coords[bit % 3] >> bit // 3 & 1) << bit)
    return leaf_ids


def partner_index(key, columns, reach, fixed_rows):
    leaf_ids = jnp.arange(LEAVES, dtype=jnp.int32)
    coords, extents = grid_coords(leaf_ids)
    offsets = jax.random.randint(key, (LEAVES, columns, 3), -reach, reach + 1).astype(jnp.int32)
    slot_ids = jnp.arange(columns)[None, :, None]
    for slot, value in fixed_rows:
        offsets = jnp.where(slot_ids == slot, jnp.full_like(offsets, value), offsets)
    moved = []
    for dim in range(3):
        moved.append(jnp.clip(coords[dim][:, None] + offsets[:, :, dim], 0, extents[dim] - 1))
    return grid_ids(moved).astype(jnp.int32)


def draw_near_index(key, part):
    return partner_index(jax.random.fold_in(key, 11), K, 1, [(0, 0)])


def draw_adm_index(key, part):
    partners = partner_index(jax.random.fold_in(key, 23), MAXC, 3, [(0, -3), (1, 3)])
    mirrored = jnp.arange(LEAVES, dtype=jnp.int32) ^ LEAVES // 2
    slot_ids = jnp.arange(MAXC)[None, :]
    return jnp.where(slot_ids == 2, mirrored[:, None], partners).astype(jnp.int32)


def draw_adm_count(key, part):
    counts = jax.random.randint(jax.random.fold_in(key, 31), (LEAVES,), 2, MAXC + 1)
    chosen = jax.random.randint(jax.random.fold_in(key, 37), (LEAVES // NPD,), 0, NPD)
    filled = (jnp.arange(NPD)[None, :] == chosen[:, None]).reshape(LEAVES)
    return jnp.where(filled, MAXC, counts).astype(jnp.int32)


def shard_levels(stream_key, extent, cuts, smallest, largest):
    def one(axis_at, parts):
        steps = jax.random.uniform(jax.random.fold_in(jax.random.fold_in(stream_key, 6), axis_at), (parts,), jnp.float32, smallest / len(cuts), largest / len(cuts))
        return jnp.repeat(jnp.exp(steps), extent[axis_at] // parts).reshape((-1,) + (1,) * (len(extent) - axis_at - 1))

    level = one(*cuts[0])
    for cut in cuts[1:]:
        level = level * one(*cut)
    return level


def scatter_about(key, shape, deviation, most, pieces=(), kind=jnp.bfloat16):
    loudness = shard_levels(key, shape, pieces, -0.22, 0.18) if pieces else 1.0
    drawn = jax.random.normal(key, shape, jnp.float32) * deviation * loudness
    return jnp.minimum(jnp.maximum(drawn, -most), most).astype(kind)


def setup_inputs(seed: int = 0) -> dict:
    streams_of = jax.random.split(jax.random.key(seed), 13)
    near_blocks = scatter_about(streams_of[0], (LEAVES, K, LEAF, LEAF), (K * LEAF) ** -0.5, 0.125, ((0, 128),))
    near_index = draw_near_index(jax.random.fold_in(streams_of[12], 71), 0)
    test_vectors = scatter_about(streams_of[2], (LEAVES, RANK, LEAF), 1.0, 6.0, ((0, 128),))
    samples = scatter_about(streams_of[3], (LEAVES, RANK, LEAF), 1.0, 6.0, ((0, 128),))
    leaf_basis = scatter_about(streams_of[4], (LEAVES, RANK, LEAF), LEAF ** -0.5, 0.375, ((0, 128),))
    col_weights = scatter_about(streams_of[5], (LEAVES, RANK, RANK), RANK ** -0.5, 0.75, ((0, 128),))
    coupling = scatter_about(streams_of[6], (LEAVES, RANK, MAXC * RANK), 1.0, 6.0, ((0, 128),))
    adm_index = draw_adm_index(jax.random.fold_in(streams_of[12], 71), 0)
    adm_count = draw_adm_count(jax.random.fold_in(streams_of[12], 71), 0)
    leaf_transfer = scatter_about(streams_of[9], (LEAVES, RANK, RANK), RANK ** -0.5, 0.75, ((0, 128),))
    inner_transfer = scatter_about(streams_of[10], (DEVICES, NPD - 1, RANK, RANK), RANK ** -0.5, 0.75, ((0, 128),))
    upper_transfer = scatter_about(streams_of[11], (DEVICES - 2, RANK, RANK), RANK ** -0.5, 0.75)
    return dict(near_blocks=near_blocks, near_index=near_index, test_vectors=test_vectors, samples=samples, leaf_basis=leaf_basis, col_weights=col_weights, coupling=coupling, adm_index=adm_index, adm_count=adm_count, leaf_transfer=leaf_transfer, inner_transfer=inner_transfer, upper_transfer=upper_transfer)


PRECISE = lax.Precision.HIGHEST

def upper_factor(gram):
    return jnp.swapaxes(jnp.linalg.cholesky(gram), -1, -2)

def merge_pairs(factors, transfer):
    weighted = jnp.einsum('nab,nbc->nac', factors, transfer.astype(jnp.float32), precision=PRECISE)
    gram = jnp.einsum('nab,nac->nbc', weighted, weighted, precision=PRECISE)
    identity = jnp.eye(RANK, dtype=jnp.float32)
    return upper_factor(0.5 * (gram[0::2] + gram[1::2]) + identity)

def reference(near_blocks, near_index, test_vectors, samples, leaf_basis, col_weights, coupling, adm_index, adm_count, leaf_transfer, inner_transfer, upper_transfer):
    identity = jnp.eye(RANK, dtype=jnp.float32)

    def leaf_factor(leaf_id):
        vectors = test_vectors[near_index[leaf_id]].astype(jnp.float32)
        near_part = jnp.einsum('krq,kpq->rp', vectors, near_blocks[leaf_id].astype(jnp.float32))
        far_sample = (samples[leaf_id].astype(jnp.float32) - near_part).astype(jnp.bfloat16)
        projected = jnp.dot(leaf_basis[leaf_id].astype(jnp.float32), far_sample.T.astype(jnp.float32), preferred_element_type=jnp.float32) * RANK ** (-0.5)
        slot_live = jnp.arange(MAXC) < adm_count[leaf_id]
        partner_weights = jnp.where(slot_live[:, None, None], col_weights[adm_index[leaf_id]].astype(jnp.float32), jnp.zeros((), jnp.float32))
        blocks = coupling[leaf_id].astype(jnp.float32).reshape(RANK, MAXC, RANK)
        coupled = jnp.einsum('rsc,sce->rse', blocks, partner_weights, precision=PRECISE)
        gram = jnp.dot(projected.T, projected, precision=PRECISE)
        gram = gram + jnp.einsum('rse,rsf->ef', coupled, coupled, precision=PRECISE) / (RANK * MAXC) + identity
        return upper_factor(gram)
    leaf_factors = lax.map(leaf_factor, jnp.arange(LEAVES))
    current = leaf_factors
    transfer = leaf_transfer
    inner = []
    for level in range(1, NPD.bit_length()):
        current = merge_pairs(current, transfer)
        count_now = NPD >> level
        inner.append(current.reshape(DEVICES, count_now, RANK, RANK))
        start = NPD - (NPD >> level - 1)
        transfer = inner_transfer[:, start:start + count_now].reshape(DEVICES * count_now, RANK, RANK)
    inner_factors = jnp.concatenate(inner, axis=1)
    ancestors = []
    for level in range(1, UP + 1):
        current = merge_pairs(current, transfer)
        ancestors.append(current[jnp.arange(DEVICES) >> level])
        if level < UP:
            start = DEVICES - (DEVICES >> level - 1)
            transfer = upper_transfer[start:start + (DEVICES >> level)]
    upper_factors = jnp.stack(ancestors, axis=1)
    return (leaf_factors, inner_factors, upper_factors)
```

```python
import jax
import jax.numpy as jnp
from jax import lax
from jax.experimental import pallas as pl
from jax.experimental.pallas import tpu as pltpu
from jax.sharding import PartitionSpec as P

PRECISE = lax.Precision.HIGHEST
AXES = ("leaf", "near")
HOPS = (1, 2, 6, 8, 24, 32, 96)
RANK = 64


def split_three(x):
    hi = x.astype(jnp.bfloat16)
    rest = x - hi.astype(jnp.float32)
    mid = rest.astype(jnp.bfloat16)
    return hi, mid, (rest - mid.astype(jnp.float32)).astype(jnp.bfloat16)


def dot32(a, b):
    return jnp.dot(a, b, preferred_element_type=jnp.float32)


def congruence(gram, transfer):
    across = jnp.transpose(transfer.astype(jnp.float32)).astype(jnp.bfloat16)
    hi, mid, low = split_three(gram)
    half = dot32(hi, transfer) + (dot32(mid, transfer) + dot32(low, transfer))
    hi, mid, low = split_three(half)
    return dot32(across, hi) + (dot32(across, mid) + dot32(across, low))


def unit_matrix():
    rows = lax.broadcasted_iota(jnp.int32, (RANK, RANK), 0)
    cols = lax.broadcasted_iota(jnp.int32, (RANK, RANK), 1)
    return (rows == cols).astype(jnp.float32)


def factor_panels(matrices):
    shape = (8, RANK)
    work = [list(panels) for panels in matrices]
    rows = lax.broadcasted_iota(jnp.int32, shape, 0)
    cols = lax.broadcasted_iota(jnp.int32, shape, 1)
    factors = [[None] * 8 for _ in work]
    for step in range(8):
        base = 8 * step
        for panels, factor in zip(work, factors):
            panel = panels[step]
            column = [
                jnp.broadcast_to(panel[:, base + k : base + k + 1], shape) for k in range(8)
            ]
            weights = [
                [jnp.broadcast_to(lower[:, base + k : base + k + 1], shape) for k in range(8)]
                for lower in panels[step + 1 :]
            ]
            rows_out = jnp.zeros(shape, jnp.float32)
            for j in range(8):
                here = rows == j
                pivot = jnp.broadcast_to(column[j][j : j + 1, :], shape)
                panel_row = jnp.broadcast_to(panel[j : j + 1, :], shape)
                rows_out = jnp.where(here, panel_row * lax.rsqrt(pivot), rows_out)
                inverse = 1.0 / pivot
                scale = column[j] * inverse
                for k in range(j + 1, 8):
                    entry = jnp.broadcast_to(column[k][j : j + 1, :], shape)
                    column[k] = jnp.where(here, entry * inverse, column[k] - scale * entry)
                panel = jnp.where(here, panel_row * inverse, panel - scale * panel_row)
            factor[step] = jnp.where(cols >= rows + base, rows_out, 0.0)
            for at, weight in enumerate(weights):
                lower = panels[step + 1 + at]
                for k in range(8):
                    lower = lower - weight[k] * jnp.broadcast_to(panel[k : k + 1, :], shape)
                panels[step + 1 + at] = lower
    return factors


def factor_kernel(grams, factors):
    count = grams.shape[0]
    out = factor_panels([[grams[b, 8 * p : 8 * p + 8, :] for p in range(8)] for b in range(count)])
    for b in range(count):
        for p in range(8):
            factors[b, 8 * p : 8 * p + 8, :] = out[b][p]


def factor(grams):
    return pl.pallas_call(
        factor_kernel, out_shape=jax.ShapeDtypeStruct(grams.shape, jnp.float32), name="factor"
    )(grams)


def local_kernel(leaf_grams, leaf_transfer, inner_transfer, inner_grams, sent):
    unit = unit_matrix()
    moved = [congruence(leaf_grams[i], leaf_transfer[i]) for i in range(4)]
    first = 0.5 * (moved[0] + moved[1]) + unit
    second = 0.5 * (moved[2] + moved[3]) + unit
    inner_grams[0] = first
    inner_grams[1] = second
    top = 0.5 * (congruence(first, inner_transfer[0, 0]) + congruence(second, inner_transfer[0, 1]))
    top = top + unit
    inner_grams[2] = top
    sent[...] = congruence(top, inner_transfer[0, 2])


def local_levels(leaf_grams, leaf_transfer, inner_transfer):
    return pl.pallas_call(
        local_kernel,
        out_shape=(
            jax.ShapeDtypeStruct((3, RANK, RANK), jnp.float32),
            jax.ShapeDtypeStruct((RANK, RANK), jnp.float32),
        ),
        name="local_levels",
    )(leaf_grams, leaf_transfer, inner_transfer)


def merge_kernel(at, own, other, transfer, gram, sent):
    merged = 0.5 * (own[...] + other[...]) + unit_matrix()
    gram[...] = merged
    sent[...] = congruence(merged, transfer[0])


def merge(at, own, other, upper_transfer):
    whole = pl.BlockSpec((RANK, RANK), lambda i, at: (0, 0))
    return pl.pallas_call(
        merge_kernel,
        grid_spec=pltpu.PrefetchScalarGridSpec(
            num_scalar_prefetch=1,
            grid=(1,),
            in_specs=[
                whole,
                whole,
                pl.BlockSpec((1, RANK, RANK), lambda i, at: (at[0], 0, 0)),
            ],
            out_specs=[whole, whole],
        ),
        out_shape=[jax.ShapeDtypeStruct((RANK, RANK), jnp.float32)] * 2,
        name="merge",
    )(at.reshape(1), own, other, upper_transfer)


def last_kernel(own, other, factor_out):
    merged = 0.5 * (own[...] + other[...]) + unit_matrix()
    out = factor_panels([[merged[8 * p : 8 * p + 8, :] for p in range(8)]])
    for p in range(8):
        factor_out[0, 8 * p : 8 * p + 8, :] = out[0][p]


def body(
    near_blocks,
    near_index,
    test_vectors,
    samples,
    leaf_basis,
    col_weights,
    coupling,
    adm_index,
    adm_count,
    leaf_transfer,
    inner_transfer,
    upper_transfer,
):
    count_local, rank_size, leaf_size = test_vectors.shape
    slot_total = adm_index.shape[1]
    weight_lines = rank_size * rank_size // leaf_size
    identity = jnp.eye(rank_size, dtype=jnp.float32)
    near_size = lax.axis_size("near")
    devices = lax.axis_size("leaf") * near_size
    total_levels = devices.bit_length() - 1
    device = lax.axis_index("leaf") * near_size + lax.axis_index("near")
    packed = jnp.concatenate(
        [test_vectors, col_weights.reshape(count_local, weight_lines, leaf_size)], axis=1
    )
    everything = lax.all_gather(packed, AXES, axis=0, tiled=True)
    neighbours = jnp.take(everything[:, :rank_size], near_index, axis=0)
    partner_lines = jnp.take(everything[:, rank_size:], adm_index, axis=0)
    near_part = jnp.einsum(
        "ikrq,ikpq->irp", neighbours, near_blocks, preferred_element_type=jnp.float32
    )
    far_sample = (samples.astype(jnp.float32) - near_part).astype(jnp.bfloat16)
    projected = jnp.einsum(
        "irp,isp->irs", leaf_basis, far_sample, preferred_element_type=jnp.float32
    ) * rank_size ** (-0.5)
    partner_weights = partner_lines.reshape(count_local, slot_total, rank_size, rank_size)
    slot_live = (jnp.arange(slot_total)[None, :] < adm_count[:, None])[:, :, None, None]
    partner_weights = jnp.where(slot_live, partner_weights, jnp.zeros((), jnp.bfloat16))
    blocks = coupling.reshape(count_local, rank_size, slot_total, rank_size)
    coupled = jnp.einsum(
        "irsc,isce->irse", blocks, partner_weights, preferred_element_type=jnp.float32
    )
    gram = jnp.einsum("iab,iac->ibc", projected, projected, precision=PRECISE)
    gram = (
        gram
        + jnp.einsum("irse,irsf->ief", coupled, coupled, precision=PRECISE)
        / (rank_size * slot_total)
        + identity
    )
    inner_grams, sent = local_levels(gram, leaf_transfer, inner_transfer)
    grams = []
    for level in range(1, total_levels + 1):
        hop = HOPS[level - 1]
        other = lax.ppermute(sent, AXES, [(d, d ^ hop) for d in range(devices)])
        if level < total_levels:
            start = devices - (devices >> level - 1)
            gram_here, sent = merge(start + (device >> level), sent, other, upper_transfer)
            grams.append(gram_here)
    root = pl.pallas_call(
        last_kernel, out_shape=jax.ShapeDtypeStruct((1, RANK, RANK), jnp.float32), name="last"
    )(sent, other)
    leaf_factors = factor(gram)
    inner_factors = factor(inner_grams)
    low = factor(jnp.stack(grams[:3]))
    high = factor(jnp.stack(grams[3:]))
    upper_factors = jnp.concatenate([low, high, root])
    return (leaf_factors, inner_factors[None], upper_factors[None])


def solution(mesh):
    split = P(AXES)
    return jax.shard_map(
        body,
        mesh=mesh,
        in_specs=(split,) * 11 + (P(),),
        out_specs=(split,) * 3,
        check_vma=False,
    )
```

```python
import jax
import jax.numpy as jnp
from jax import lax
from jax.experimental import pallas as pl
from jax.experimental.pallas import tpu as pltpu
from jax.sharding import PartitionSpec as P

AXES = ("leaf", "near")
HOPS = (1, 2, 6, 8, 24, 32, 96)
RANK = 64


def split_three(x):
    hi = x.astype(jnp.bfloat16)
    rest = x - hi.astype(jnp.float32)
    mid = rest.astype(jnp.bfloat16)
    return hi, mid, (rest - mid.astype(jnp.float32)).astype(jnp.bfloat16)


def dot32(a, b):
    return jnp.dot(a, b, preferred_element_type=jnp.float32)


def dot_last(a, b):
    return lax.dot_general(a, b, (((1,), (1,)), ((), ())), preferred_element_type=jnp.float32)


def congruence(gram, transfer):
    across = jnp.transpose(transfer.astype(jnp.float32)).astype(jnp.bfloat16)
    hi, mid, low = split_three(gram)
    half = dot32(hi, transfer) + (dot32(mid, transfer) + dot32(low, transfer))
    hi, mid, low = split_three(half)
    return dot32(across, hi) + (dot32(across, mid) + dot32(across, low))


def unit_matrix():
    rows = lax.broadcasted_iota(jnp.int32, (RANK, RANK), 0)
    cols = lax.broadcasted_iota(jnp.int32, (RANK, RANK), 1)
    return (rows == cols).astype(jnp.float32)


def factor_panels(matrices):
    shape = (8, RANK)
    work = [list(panels) for panels in matrices]
    rows = lax.broadcasted_iota(jnp.int32, shape, 0)
    cols = lax.broadcasted_iota(jnp.int32, shape, 1)
    factors = [[None] * 8 for _ in work]
    for step in range(8):
        base = 8 * step
        for panels, factor in zip(work, factors):
            panel = panels[step]
            column = [
                jnp.broadcast_to(panel[:, base + k : base + k + 1], shape) for k in range(8)
            ]
            weights = [
                [jnp.broadcast_to(lower[:, base + k : base + k + 1], shape) for k in range(8)]
                for lower in panels[step + 1 :]
            ]
            rows_out = jnp.zeros(shape, jnp.float32)
            for j in range(8):
                here = rows == j
                pivot = jnp.broadcast_to(column[j][j : j + 1, :], shape)
                panel_row = jnp.broadcast_to(panel[j : j + 1, :], shape)
                rows_out = jnp.where(here, panel_row * lax.rsqrt(pivot), rows_out)
                inverse = 1.0 / pivot
                scale = column[j] * inverse
                for k in range(j + 1, 8):
                    entry = jnp.broadcast_to(column[k][j : j + 1, :], shape)
                    column[k] = jnp.where(here, entry * inverse, column[k] - scale * entry)
                panel = jnp.where(here, panel_row * inverse, panel - scale * panel_row)
            factor[step] = jnp.where(cols >= rows + base, rows_out, 0.0)
            for at, weight in enumerate(weights):
                lower = panels[step + 1 + at]
                for k in range(8):
                    lower = lower - weight[k] * jnp.broadcast_to(panel[k : k + 1, :], shape)
                panels[step + 1 + at] = lower
    return factors


def factor_kernel(grams, factors):
    count = grams.shape[0]
    out = factor_panels([[grams[b, 8 * p : 8 * p + 8, :] for p in range(8)] for b in range(count)])
    for b in range(count):
        for p in range(8):
            factors[b, 8 * p : 8 * p + 8, :] = out[b][p]


def factor(grams):
    return pl.pallas_call(
        factor_kernel, out_shape=jax.ShapeDtypeStruct(grams.shape, jnp.float32), name="factor"
    )(grams)


RING = ((0, 1, 2), (1, 2, 0))


def chip_shift(device, stage, amount):
    core = device & 1
    axis = RING[core][stage]
    at = 1 + 2 * axis
    place = device >> at & 3
    return device - (place << at) + ((place + amount & 3) << at)


def ring_send(x, stage, amount, devices):
    return lax.ppermute(x, AXES, [(d, chip_shift(d, stage, amount)) for d in range(devices)])


def grid_places(device):
    first = (device >> 1 & 1) + 2 * (device >> 4 & 1)
    second = (device >> 2 & 1) + 2 * (device >> 5 & 1)
    third = (device & 1) + 2 * (device >> 3 & 1) + 4 * (device >> 6 & 1)
    return first, second, third


def grid_device(first, second, third):
    low = (third & 1) + 2 * (first & 1) + 4 * (second & 1) + 8 * (third >> 1 & 1)
    return low + 16 * (first >> 1) + 32 * (second >> 1) + 64 * (third >> 2)


def grid_send(x, dim, amount, devices):
    pairs = []
    for d in range(devices):
        place = list(grid_places(d))
        place[dim] += amount
        if 0 <= place[dim] < (4, 4, 8)[dim]:
            pairs.append((d, grid_device(*place)))
    return lax.ppermute(x, AXES, pairs)


def across_chips(x, devices):
    pairs = []
    for d in range(devices):
        first, second, third = grid_places(d)
        third += 1 if third & 1 else -1
        if 0 <= third < 8:
            pairs.append((d, grid_device(first, second, third)))
    return lax.ppermute(x, AXES, pairs)


def swap_cores(x, devices):
    return lax.ppermute(x, AXES, [(d, d ^ 1) for d in range(devices)])


def exchange_vectors(own, devices):
    inside = swap_cores(own, devices)
    outside = across_chips(own, devices)
    layers = jnp.stack([inside, own, outside])
    before = grid_send(layers[:, 2:4], 1, 1, devices)
    after = grid_send(layers[:, 0:2], 1, -1, devices)
    rows = jnp.concatenate([before, layers, after], axis=1)
    left = grid_send(rows[:, 1::2], 0, 1, devices)
    right = grid_send(rows[:, 0::2], 0, -1, devices)
    return [own, inside, outside, before, after, left, right]


def vector_slots(near_index, device):
    first, second, third = grid_places(device)
    cell = near_index
    x = (cell & 1) + 2 * (cell >> 3 & 1) + 4 * (cell >> 6 & 1) - 2 * first
    y = (cell >> 1 & 1) + 2 * (cell >> 4 & 1) + 4 * (cell >> 7 & 1) - 2 * second
    z = (cell >> 2 & 1) + 2 * (cell >> 5 & 1) + 4 * (cell >> 8 & 1)
    layer = jnp.where(z == third, 1, jnp.where(z >> 1 == third >> 1, 0, 2))
    start = jnp.where(layer == 1, 0, jnp.where(layer == 0, 4, 8))
    slot = start + x + 2 * y
    slot = jnp.where(y == -1, 12 + 2 * layer + x, slot)
    slot = jnp.where(y == 2, 18 + 2 * layer + x, slot)
    slot = jnp.where(x == -1, 24 + 4 * layer + y + 1, slot)
    return jnp.where(x == 2, 36 + 4 * layer + y + 1, slot)


def exchange_weights(own, devices):
    held = own
    for stage in range(2):
        parts = [ring_send(held, stage, k, devices) for k in (1, 3, 2)]
        held = jnp.concatenate([held] + parts)
    half = held.shape[0] // 2
    back = ring_send(held, 2, 1, devices)
    front = ring_send(held, 2, 3, devices)
    far_low = ring_send(back[:half], 2, 1, devices)
    far_high = ring_send(front[half:], 2, 3, devices)
    mine = [held, back, front, far_low, far_high]
    return mine + [swap_cores(x, devices) for x in mine]


def weight_tiles(adm_index, device):
    owner = adm_index >> 2
    label = []
    for axis in range(3):
        ahead = (owner >> 1 + 2 * axis) - (device >> 1 + 2 * axis) & 3
        label.append(jnp.where(ahead == 3, 1, jnp.where(ahead == 1, 2, jnp.where(ahead == 2, 3, 0))))
    order = [
        label[RING[0][2]] * 16 + label[RING[0][1]] * 4 + label[RING[0][0]],
        label[RING[1][2]] * 16 + label[RING[1][1]] * 4 + label[RING[1][0]],
    ]
    core = owner & 1
    other = core ^ (device & 1)
    return other * 128 + 2 * jnp.where(core == 1, order[1], order[0]) + (adm_index >> 1 & 1)


def load_pieces(pieces, buffer, semaphores):
    at = 0
    copies = []
    for n, piece in enumerate(pieces):
        copies.append(
            pltpu.make_async_copy(piece, buffer.at[pl.ds(at, piece.shape[0])], semaphores.at[n])
        )
        at += piece.shape[0]
    return copies


def near_kernel(slots, blocks, samples, basis, *rest):
    pieces, (gram, vectors, semaphores) = rest[:7], rest[7:]
    leaf = pl.program_id(0)

    @pl.when(leaf == 0)
    def _():
        copies = load_pieces(pieces, vectors, semaphores)
        for copy in copies:
            copy.start()
        for copy in copies:
            copy.wait()

    total = None
    for k in range(8):
        part = dot_last(vectors[slots[8 * leaf + k]], blocks[0, k])
        total = part if total is None else total + part
    far = (samples[0].astype(jnp.float32) - total).astype(jnp.bfloat16)
    scale = RANK**-0.5
    wide = dot_last(basis[0], far) * scale
    tall = dot_last(far, basis[0]) * scale
    wide_hi = wide.astype(jnp.bfloat16)
    wide_low = (wide - wide_hi.astype(jnp.float32)).astype(jnp.bfloat16)
    tall_hi = tall.astype(jnp.bfloat16)
    tall_low = (tall - tall_hi.astype(jnp.float32)).astype(jnp.bfloat16)
    gram[0] = dot32(tall_hi, wide_hi) + (dot32(tall_hi, wide_low) + dot32(tall_low, wide_hi))


def near_grams(slots, near_blocks, samples, leaf_basis, pieces):
    count, per_leaf, size, _ = near_blocks.shape
    rank = samples.shape[1]
    row = pl.BlockSpec((1, rank, size), lambda i, slots: (i, 0, 0))
    pieces = [piece.reshape(-1, rank, size) for piece in pieces]
    return pl.pallas_call(
        near_kernel,
        grid_spec=pltpu.PrefetchScalarGridSpec(
            num_scalar_prefetch=1,
            grid=(count,),
            in_specs=[
                pl.BlockSpec((1, per_leaf, size, size), lambda i, slots: (i, 0, 0, 0)),
                row,
                row,
            ]
            + [pl.BlockSpec(memory_space=pl.ANY)] * len(pieces),
            out_specs=pl.BlockSpec((1, rank, rank), lambda i, slots: (i, 0, 0)),
            scratch_shapes=[
                pltpu.VMEM((48, rank, size), jnp.bfloat16),
                pltpu.SemaphoreType.DMA((len(pieces),)),
            ],
        ),
        out_shape=jax.ShapeDtypeStruct((count, rank, rank), jnp.float32),
        name="near_grams",
    )(slots, near_blocks, samples, leaf_basis, *pieces)


def leaf_kernel(tiles, halves, coupling, near_gram, leaf_transfer, inner_transfer, *rest):
    pieces = rest[:10]
    leaf_grams, inner_grams, sent, weights, coupled, moved, semaphores = rest[10:]
    leaf = pl.program_id(0)

    @pl.when(leaf == 0)
    def _():
        copies = load_pieces(pieces, weights, semaphores)
        for copy in copies:
            copy.start()
        for copy in copies:
            copy.wait()

    side = lax.broadcasted_iota(jnp.int32, (RANK, 2 * RANK), 1) >> 6
    nothing = jnp.zeros((RANK, 2 * RANK), jnp.bfloat16)
    for pair in range(16):
        chosen = []
        for s in (2 * pair, 2 * pair + 1):
            tile = weights[tiles[32 * leaf + s]]
            chosen.append(jnp.where(side == halves[32 * leaf + s], tile, nothing))
        both = jnp.concatenate(
            [
                jnp.concatenate([chosen[0], nothing], axis=1),
                jnp.concatenate([nothing, chosen[1]], axis=1),
            ],
            axis=0,
        )
        product = dot32(coupling[0, :, 128 * pair : 128 * pair + 128], both).astype(jnp.bfloat16)
        coupled[128 * pair : 128 * pair + 64, :] = product[:, :128]
        coupled[128 * pair + 64 : 128 * pair + 128, :] = product[:, 128:]
    square = lax.dot_general(
        coupled[...], coupled[...], (((0,), (0,)), ((), ())), preferred_element_type=jnp.float32
    )
    sums = square[:RANK, :RANK] + square[RANK:, RANK:]
    unit = unit_matrix()
    gram = near_gram[0] + sums * (1.0 / 2048) + unit
    leaf_grams[leaf] = gram
    moved[leaf] = congruence(gram, leaf_transfer[leaf])

    @pl.when(leaf == 3)
    def _():
        first = 0.5 * (moved[0] + moved[1]) + unit
        second = 0.5 * (moved[2] + moved[3]) + unit
        inner_grams[0] = first
        inner_grams[1] = second
        top = congruence(first, inner_transfer[0, 0]) + congruence(second, inner_transfer[0, 1])
        top = 0.5 * top + unit
        inner_grams[2] = top
        sent[...] = congruence(top, inner_transfer[0, 2])


def leaf_levels(tiles, halves, coupling, near_gram, leaf_transfer, inner_transfer, pieces):
    count, rank, width = coupling.shape
    f32 = jnp.float32
    return pl.pallas_call(
        leaf_kernel,
        grid_spec=pltpu.PrefetchScalarGridSpec(
            num_scalar_prefetch=2,
            grid=(count,),
            in_specs=[
                pl.BlockSpec((1, rank, width), lambda i, *_: (i, 0, 0)),
                pl.BlockSpec((1, rank, rank), lambda i, *_: (i, 0, 0)),
                pl.BlockSpec((count, rank, rank), lambda i, *_: (0, 0, 0)),
                pl.BlockSpec((1, count - 1, rank, rank), lambda i, *_: (0, 0, 0, 0)),
            ]
            + [pl.BlockSpec(memory_space=pl.ANY)] * len(pieces),
            out_specs=[
                pl.BlockSpec((count, rank, rank), lambda i, *_: (0, 0, 0)),
                pl.BlockSpec((count - 1, rank, rank), lambda i, *_: (0, 0, 0)),
                pl.BlockSpec((rank, rank), lambda i, *_: (0, 0)),
            ],
            scratch_shapes=[
                pltpu.VMEM((256, rank, 2 * rank), jnp.bfloat16),
                pltpu.VMEM((width, 2 * rank), jnp.bfloat16),
                pltpu.VMEM((count, rank, rank), f32),
                pltpu.SemaphoreType.DMA((len(pieces),)),
            ],
        ),
        out_shape=[
            jax.ShapeDtypeStruct((count, rank, rank), f32),
            jax.ShapeDtypeStruct((count - 1, rank, rank), f32),
            jax.ShapeDtypeStruct((rank, rank), f32),
        ],
        name="leaf_levels",
    )(tiles, halves, coupling, near_gram, leaf_transfer, inner_transfer, *pieces)


def merge_kernel(at, own, other, transfer, gram, sent):
    merged = 0.5 * (own[...] + other[...]) + unit_matrix()
    gram[...] = merged
    sent[...] = congruence(merged, transfer[0])


def merge(at, own, other, upper_transfer):
    whole = pl.BlockSpec((RANK, RANK), lambda i, at: (0, 0))
    return pl.pallas_call(
        merge_kernel,
        grid_spec=pltpu.PrefetchScalarGridSpec(
            num_scalar_prefetch=1,
            grid=(1,),
            in_specs=[
                whole,
                whole,
                pl.BlockSpec((1, RANK, RANK), lambda i, at: (at[0], 0, 0)),
            ],
            out_specs=[whole, whole],
        ),
        out_shape=[jax.ShapeDtypeStruct((RANK, RANK), jnp.float32)] * 2,
        name="merge",
    )(at.reshape(1), own, other, upper_transfer)


def last_kernel(own, other, factor_out):
    merged = 0.5 * (own[...] + other[...]) + unit_matrix()
    out = factor_panels([[merged[8 * p : 8 * p + 8, :] for p in range(8)]])
    for p in range(8):
        factor_out[0, 8 * p : 8 * p + 8, :] = out[0][p]


def body(
    near_blocks,
    near_index,
    test_vectors,
    samples,
    leaf_basis,
    col_weights,
    coupling,
    adm_index,
    adm_count,
    leaf_transfer,
    inner_transfer,
    upper_transfer,
):
    count, rank, size = test_vectors.shape
    slots = adm_index.shape[1]
    devices = lax.axis_size("leaf") * lax.axis_size("near")
    total_levels = devices.bit_length() - 1
    device = lax.axis_index("leaf") * lax.axis_size("near") + lax.axis_index("near")
    paired = jnp.concatenate([col_weights[0::2], col_weights[1::2]], axis=2)
    weights = exchange_weights(paired, devices)
    vectors = exchange_vectors(test_vectors, devices)
    near_gram = near_grams(
        vector_slots(near_index, device).reshape(-1), near_blocks, samples, leaf_basis, vectors
    )
    live = jnp.arange(slots)[None, :] < adm_count[:, None]
    halves = jnp.where(live, adm_index & 1, 2)
    gram, inner_grams, sent = leaf_levels(
        weight_tiles(adm_index, device).reshape(-1),
        halves.reshape(-1),
        coupling,
        near_gram,
        leaf_transfer,
        inner_transfer,
        weights,
    )
    grams = []
    for level in range(1, total_levels + 1):
        hop = HOPS[level - 1]
        other = lax.ppermute(sent, AXES, [(d, d ^ hop) for d in range(devices)])
        if level < total_levels:
            start = devices - (devices >> level - 1)
            gram_here, sent = merge(start + (device >> level), sent, other, upper_transfer)
            grams.append(gram_here)
    root = pl.pallas_call(
        last_kernel, out_shape=jax.ShapeDtypeStruct((1, RANK, RANK), jnp.float32), name="last"
    )(sent, other)
    leaf_factors = factor(gram)
    inner_factors = factor(inner_grams)
    low = factor(jnp.stack(grams[:3]))
    high = factor(jnp.stack(grams[3:]))
    upper_factors = jnp.concatenate([low, high, root])
    return (leaf_factors, inner_factors[None], upper_factors[None])


def solution(mesh):
    split = P(AXES)
    return jax.shard_map(
        body,
        mesh=mesh,
        in_specs=(split,) * 11 + (P(),),
        out_specs=(split,) * 3,
        check_vma=False,
    )
```

```python
import functools

import jax
import jax.numpy as jnp
from jax import lax
from jax.experimental import pallas as pl
from jax.experimental.pallas import tpu as pltpu
from jax.sharding import PartitionSpec as P

AXES = ("leaf", "near")
HOPS = (1, 2, 6, 8, 24, 32, 96)
RANK = 64


def split_three(x):
    hi = x.astype(jnp.bfloat16)
    rest = x - hi.astype(jnp.float32)
    mid = rest.astype(jnp.bfloat16)
    return hi, mid, (rest - mid.astype(jnp.float32)).astype(jnp.bfloat16)


def dot32(a, b):
    return jnp.dot(a, b, preferred_element_type=jnp.float32)


def dot_last(a, b):
    return lax.dot_general(a, b, (((1,), (1,)), ((), ())), preferred_element_type=jnp.float32)


def congruence(gram, transfer):
    across = jnp.transpose(transfer.astype(jnp.float32)).astype(jnp.bfloat16)
    hi, mid, low = split_three(gram)
    half = dot32(hi, transfer) + (dot32(mid, transfer) + dot32(low, transfer))
    hi, mid, low = split_three(half)
    return dot32(across, hi) + (dot32(across, mid) + dot32(across, low))


def unit_matrix():
    rows = lax.broadcasted_iota(jnp.int32, (RANK, RANK), 0)
    cols = lax.broadcasted_iota(jnp.int32, (RANK, RANK), 1)
    return (rows == cols).astype(jnp.float32)


def factor_panels(matrices):
    shape = (8, RANK)
    work = [list(panels) for panels in matrices]
    rows = lax.broadcasted_iota(jnp.int32, shape, 0)
    cols = lax.broadcasted_iota(jnp.int32, shape, 1)
    factors = [[None] * 8 for _ in work]
    for step in range(8):
        base = 8 * step
        for panels, factor in zip(work, factors):
            panel = panels[step]
            column = [
                jnp.broadcast_to(panel[:, base + k : base + k + 1], shape) for k in range(8)
            ]
            weights = [
                [jnp.broadcast_to(lower[:, base + k : base + k + 1], shape) for k in range(8)]
                for lower in panels[step + 1 :]
            ]
            rows_out = jnp.zeros(shape, jnp.float32)
            for j in range(8):
                here = rows == j
                pivot = jnp.broadcast_to(column[j][j : j + 1, :], shape)
                panel_row = jnp.broadcast_to(panel[j : j + 1, :], shape)
                rows_out = jnp.where(here, panel_row * lax.rsqrt(pivot), rows_out)
                inverse = 1.0 / pivot
                scale = column[j] * inverse
                for k in range(j + 1, 8):
                    entry = jnp.broadcast_to(column[k][j : j + 1, :], shape)
                    column[k] = jnp.where(here, entry * inverse, column[k] - scale * entry)
                panel = jnp.where(here, panel_row * inverse, panel - scale * panel_row)
            factor[step] = jnp.where(cols >= rows + base, rows_out, 0.0)
            for at, weight in enumerate(weights):
                lower = panels[step + 1 + at]
                for k in range(8):
                    lower = lower - weight[k] * jnp.broadcast_to(panel[k : k + 1, :], shape)
                panels[step + 1 + at] = lower
    return factors


def in_vmem(x):
    return pltpu.with_memory_space_constraint(x, pltpu.VMEM)


def panels_of(matrix):
    return [matrix[8 * p : 8 * p + 8, :] for p in range(8)]


def factor_kernel(leaf_grams, inner_grams, leaf_factors, inner_factors):
    count = leaf_grams.shape[0]
    grams = [leaf_grams[n] for n in range(count)] + [inner_grams[n] for n in range(count - 1)]
    for n, panels in enumerate(factor_panels([panels_of(gram) for gram in grams])):
        for p in range(8):
            if n < count:
                leaf_factors[n, 8 * p : 8 * p + 8, :] = panels[p]
            else:
                inner_factors[n - count, 8 * p : 8 * p + 8, :] = panels[p]


def factor_local(leaf_grams, inner_grams):
    return pl.pallas_call(
        factor_kernel,
        in_specs=[pl.BlockSpec(memory_space=pltpu.VMEM)] * 2,
        out_shape=[
            jax.ShapeDtypeStruct(leaf_grams.shape, jnp.float32),
            jax.ShapeDtypeStruct(inner_grams.shape, jnp.float32),
        ],
        compiler_params=limit(4),
        name="factor_local",
    )(in_vmem(leaf_grams), in_vmem(inner_grams))


RING = ((0, 1, 2), (1, 2, 0))


def ring_swap(x, stage, flip, devices):
    pairs = [(d, d ^ flip << 1 + 2 * RING[d & 1][stage]) for d in range(devices)]
    return lax.ppermute(x, AXES, pairs)


def grid_places(device):
    first = (device >> 1 & 1) + 2 * (device >> 4 & 1)
    second = (device >> 2 & 1) + 2 * (device >> 5 & 1)
    third = (device & 1) + 2 * (device >> 3 & 1) + 4 * (device >> 6 & 1)
    return first, second, third


def grid_device(first, second, third):
    low = (third & 1) + 2 * (first & 1) + 4 * (second & 1) + 8 * (third >> 1 & 1)
    return low + 16 * (first >> 1) + 32 * (second >> 1) + 64 * (third >> 2)


def grid_swap(x, dim, shift, devices):
    pairs = []
    for d in range(devices):
        place = list(grid_places(d))
        to = place[dim] + (1 if place[dim] % 2 == shift else -1)
        if 0 <= to < (4, 4, 8)[dim]:
            place[dim] = to
        pairs.append((d, grid_device(*place)))
    return lax.ppermute(x, AXES, pairs)


def neighbours(lower, upper, dim, odd, devices):
    even_pairs = grid_swap(jnp.where(odd, lower, upper), dim, 0, devices)
    odd_pairs = grid_swap(jnp.where(odd, upper, lower), dim, 1, devices)
    return jnp.where(odd, even_pairs, odd_pairs), jnp.where(odd, odd_pairs, even_pairs)


def swap_cores(x, devices):
    return lax.ppermute(x, AXES, [(d, d ^ 1) for d in range(devices)])


def exchange_vectors(own, device, devices):
    first, second, _ = grid_places(device)
    left, right = neighbours(own[0::2], own[1::2], 0, first % 2 == 1, devices)
    rows = jnp.stack([left, own[0::2], own[1::2], right], axis=1)
    before, after = neighbours(rows[0], rows[1], 1, second % 2 == 1, devices)
    plane = jnp.concatenate([before, rows[0], rows[1], after])
    return [plane, swap_cores(plane, devices), grid_swap(plane, 2, 1, devices)]


def vector_slots(near_index, device):
    first, second, third = grid_places(device)
    cell = near_index
    x = (cell & 1) + 2 * (cell >> 3 & 1) + 4 * (cell >> 6 & 1) - 2 * first
    y = (cell >> 1 & 1) + 2 * (cell >> 4 & 1) + 4 * (cell >> 7 & 1) - 2 * second
    z = (cell >> 2 & 1) + 2 * (cell >> 5 & 1) + 4 * (cell >> 8 & 1)
    plane = jnp.where(z == third, 0, jnp.where(z >> 1 == third >> 1, 1, 2))
    return 16 * plane + 4 * (y + 1) + x + 1


def gather_weights(own, devices):
    held = own
    for stage in range(2):
        for flip in (1, 3):
            held = jnp.concatenate([held, ring_swap(held, stage, flip, devices)])
    near = ring_swap(held, 2, 1, devices)
    last = ring_swap(held, 2, 3, devices)
    return [held, near, last]


def gather_far(near, last, devices):
    half = near.shape[0] // 2
    return [ring_swap(last[:half], 2, 1, devices), ring_swap(near[half:], 2, 3, devices)]


def weight_tiles(adm_index, device):
    owner = adm_index >> 2
    label = []
    for axis in range(3):
        apart = (owner ^ device) >> 1 + 2 * axis & 3
        label.append(apart ^ apart >> 1)
    order = [
        label[RING[0][2]] * 16 + label[RING[0][1]] * 4 + label[RING[0][0]],
        label[RING[1][2]] * 16 + label[RING[1][1]] * 4 + label[RING[1][0]],
    ]
    core = owner & 1
    other = core ^ (device & 1)
    return other * 128 + 2 * jnp.where(core == 1, order[1], order[0]) + (adm_index >> 1 & 1)


def join_pieces(pieces, buffer):
    at = 0
    for piece in pieces:
        buffer[at : at + piece.shape[0]] = piece[...]
        at += piece.shape[0]


def limit(mebibytes):
    return pltpu.CompilerParams(vmem_limit_bytes=mebibytes << 20)


def near_kernel(slots, blocks, samples, basis, *rest):
    pieces, (gram, vectors) = rest[:3], rest[3:]
    join_pieces(pieces, vectors)
    for leaf in range(blocks.shape[0]):
        near_leaf(leaf, slots, blocks, samples, basis, vectors, gram)


def near_leaf(leaf, slots, blocks, samples, basis, vectors, gram):
    total = None
    for k in range(8):
        part = dot_last(vectors[slots[8 * leaf + k]], blocks[leaf, k])
        total = part if total is None else total + part
    far = (samples[leaf].astype(jnp.float32) - total).astype(jnp.bfloat16)
    scale = RANK**-0.5
    wide = dot_last(basis[leaf], far) * scale
    tall = dot_last(far, basis[leaf]) * scale
    wide_hi = wide.astype(jnp.bfloat16)
    wide_low = (wide - wide_hi.astype(jnp.float32)).astype(jnp.bfloat16)
    tall_hi = tall.astype(jnp.bfloat16)
    tall_low = (tall - tall_hi.astype(jnp.float32)).astype(jnp.bfloat16)
    gram[leaf] = dot32(tall_hi, wide_hi) + (dot32(tall_hi, wide_low) + dot32(tall_low, wide_hi))


def near_grams(slots, near_blocks, samples, leaf_basis, pieces):
    count, rank, size = samples.shape
    vmem = pl.BlockSpec(memory_space=pltpu.VMEM)
    return pl.pallas_call(
        near_kernel,
        in_specs=[pl.BlockSpec(memory_space=pltpu.SMEM)] + [vmem] * (3 + len(pieces)),
        out_specs=vmem,
        out_shape=pltpu.VMEM((count, rank, rank), jnp.float32),
        scratch_shapes=[pltpu.VMEM((48, rank, size), jnp.bfloat16)],
        compiler_params=limit(8),
        name="near_grams",
    )(
        slots,
        in_vmem(near_blocks),
        in_vmem(samples),
        in_vmem(leaf_basis),
        *[in_vmem(piece) for piece in pieces],
    )


def select_kernel(nodes, upper_transfer, transfers, semaphores):
    copies = [
        pltpu.make_async_copy(upper_transfer.at[nodes[n]], transfers.at[n], semaphores.at[n])
        for n in range(transfers.shape[0])
    ]
    for copy in copies:
        copy.start()
    for copy in copies:
        copy.wait()


def select_transfers(nodes, upper_transfer):
    levels, rank = nodes.shape[0], upper_transfer.shape[1]
    return pl.pallas_call(
        select_kernel,
        in_specs=[
            pl.BlockSpec(memory_space=pltpu.SMEM),
            pl.BlockSpec(memory_space=pl.ANY),
        ],
        out_specs=pl.BlockSpec(memory_space=pltpu.VMEM),
        out_shape=pltpu.VMEM((levels, rank, rank), jnp.bfloat16),
        scratch_shapes=[pltpu.SemaphoreType.DMA((levels,))],
        compiler_params=limit(4),
        name="select_transfers",
    )(nodes, upper_transfer)


def leaf_kernel(tiles, halves, coupling, near_gram, leaf_transfer, inner_transfer, *rest):
    pieces, (leaf_grams, inner_grams, sent, weights, coupled) = rest[:10], rest[10:]
    join_pieces(pieces, weights)
    unit = unit_matrix()
    moved = []
    for leaf in range(leaf_grams.shape[0]):
        sums = coupled_gram(leaf, tiles, halves, coupling, weights, coupled.at[leaf % 2])
        gram = near_gram[leaf] + sums * (1.0 / 2048) + unit
        leaf_grams[leaf] = gram
        moved.append(congruence(gram, leaf_transfer[leaf]))
    first = 0.5 * (moved[0] + moved[1]) + unit
    second = 0.5 * (moved[2] + moved[3]) + unit
    inner_grams[0] = first
    inner_grams[1] = second
    top = congruence(first, inner_transfer[0, 0]) + congruence(second, inner_transfer[0, 1])
    top = 0.5 * top + unit
    inner_grams[2] = top
    sent[...] = congruence(top, inner_transfer[0, 2])


def coupled_gram(leaf, tiles, halves, coupling, weights, coupled):
    side = lax.broadcasted_iota(jnp.int32, (RANK, 2 * RANK), 1) >> 6
    nothing = jnp.zeros((RANK, 2 * RANK), jnp.bfloat16)
    for pair in range(16):
        chosen = []
        for s in (2 * pair, 2 * pair + 1):
            tile = weights[tiles[32 * leaf + s]]
            chosen.append(jnp.where(side == halves[32 * leaf + s], tile, nothing))
        both = jnp.concatenate(
            [
                jnp.concatenate([chosen[0], nothing], axis=1),
                jnp.concatenate([nothing, chosen[1]], axis=1),
            ],
            axis=0,
        )
        product = dot32(coupling[leaf, :, 128 * pair : 128 * pair + 128], both).astype(jnp.bfloat16)
        coupled[128 * pair : 128 * pair + 64, :] = product[:, :128]
        coupled[128 * pair + 64 : 128 * pair + 128, :] = product[:, 128:]
    square = lax.dot_general(
        coupled[...], coupled[...], (((0,), (0,)), ((), ())), preferred_element_type=jnp.float32
    )
    return square[:RANK, :RANK] + square[RANK:, RANK:]


def leaf_levels(tiles, halves, coupling, near_gram, leaf_transfer, inner_transfer, pieces):
    count, rank, width = coupling.shape
    vmem = pl.BlockSpec(memory_space=pltpu.VMEM)
    inputs = [coupling, near_gram, leaf_transfer, inner_transfer] + list(pieces)
    return pl.pallas_call(
        leaf_kernel,
        in_specs=[pl.BlockSpec(memory_space=pltpu.SMEM)] * 2 + [vmem] * len(inputs),
        out_specs=[vmem] * 3,
        out_shape=[
            pltpu.VMEM((count, rank, rank), jnp.float32),
            pltpu.VMEM((count - 1, rank, rank), jnp.float32),
            pltpu.VMEM((rank, rank), jnp.float32),
        ],
        scratch_shapes=[
            pltpu.VMEM((256, rank, 2 * rank), jnp.bfloat16),
            pltpu.VMEM((2, width, 2 * rank), jnp.bfloat16),
        ],
        compiler_params=limit(12),
        name="leaf_levels",
    )(tiles, halves, *[in_vmem(x) for x in inputs])


def merge_kernel(level, own, other, transfers, gram, sent):
    merged = 0.5 * (own[...] + other[...]) + unit_matrix()
    gram[...] = merged
    sent[...] = congruence(merged, transfers[level])


def merge(level, own, other, transfers):
    return pl.pallas_call(
        functools.partial(merge_kernel, level),
        in_specs=[pl.BlockSpec(memory_space=pltpu.VMEM)] * 3,
        out_specs=[pl.BlockSpec(memory_space=pltpu.VMEM)] * 2,
        out_shape=[pltpu.VMEM((RANK, RANK), jnp.float32)] * 2,
        compiler_params=limit(4),
        name="merge",
    )(in_vmem(own), in_vmem(other), in_vmem(transfers))


def last_kernel(own, other, *rest):
    grams, factors = rest[:-1], rest[-1]
    merged = 0.5 * (own[...] + other[...]) + unit_matrix()
    out = factor_panels([panels_of(gram[...]) for gram in grams] + [panels_of(merged)])
    for n, panels in enumerate(out):
        for p in range(8):
            factors[n, 8 * p : 8 * p + 8, :] = panels[p]


def factor_upper(own, other, grams):
    count = len(grams) + 1
    return pl.pallas_call(
        last_kernel,
        in_specs=[pl.BlockSpec(memory_space=pltpu.VMEM)] * (count + 1),
        out_shape=jax.ShapeDtypeStruct((count, RANK, RANK), jnp.float32),
        compiler_params=limit(4),
        name="factor_upper",
    )(in_vmem(own), in_vmem(other), *[in_vmem(gram) for gram in grams])


def body(
    near_blocks,
    near_index,
    test_vectors,
    samples,
    leaf_basis,
    col_weights,
    coupling,
    adm_index,
    adm_count,
    leaf_transfer,
    inner_transfer,
    upper_transfer,
):
    count, rank, size = test_vectors.shape
    slots = adm_index.shape[1]
    devices = lax.axis_size("leaf") * lax.axis_size("near")
    total_levels = devices.bit_length() - 1
    device = lax.axis_index("leaf") * lax.axis_size("near") + lax.axis_index("near")
    paired = jnp.concatenate([col_weights[0::2], col_weights[1::2]], axis=2)
    weights = gather_weights(paired, devices)
    vectors = exchange_vectors(test_vectors, device, devices)
    levels = jnp.arange(1, total_levels)
    nodes = devices - (devices >> levels - 1) + (device >> levels)
    held, upper_transfer = lax.optimization_barrier((weights[0], upper_transfer))
    transfers = select_transfers(nodes, upper_transfer)
    live = jnp.arange(slots)[None, :] < adm_count[:, None]
    halves = jnp.where(live, adm_index & 1, 2).reshape(-1)
    tiles = weight_tiles(adm_index, device).reshape(-1)
    wanted = vector_slots(near_index, device).reshape(-1)
    near, last, transfers, halves, tiles, wanted = lax.optimization_barrier(
        (weights[1], weights[2], transfers, halves, tiles, wanted)
    )
    far = gather_far(near, last, devices)
    weights = [held, near, last]
    swapped = [swap_cores(piece, devices) for piece in weights]
    near_gram = near_grams(wanted, near_blocks, samples, leaf_basis, vectors)
    far_low, far_high, near_gram = lax.optimization_barrier((far[0], far[1], near_gram))
    far = [far_low, far_high]
    weights = weights + far + swapped + [swap_cores(piece, devices) for piece in far]
    gram, inner_grams, sent = leaf_levels(
        tiles,
        halves,
        coupling,
        near_gram,
        leaf_transfer,
        inner_transfer,
        weights,
    )
    grams = []
    for level in range(1, total_levels + 1):
        hop = HOPS[level - 1]
        other = lax.ppermute(sent, AXES, [(d, d ^ hop) for d in range(devices)])
        if level == 1:
            local_factors = factor_local(gram, inner_grams)
            other, local_factors = lax.optimization_barrier((other, local_factors))
        if level < total_levels:
            gram_here, sent = merge(level - 1, sent, other, transfers)
            grams.append(gram_here)
    upper_factors = factor_upper(sent, other, grams)
    leaf_factors, inner_factors = local_factors
    return (leaf_factors, inner_factors[None], upper_factors[None])


def solution(mesh):
    split = P(AXES)
    return jax.shard_map(
        body,
        mesh=mesh,
        in_specs=(split,) * 11 + (P(),),
        out_specs=(split,) * 3,
        check_vma=False,
    )
```

```python
import functools

import jax
import jax.numpy as jnp
from jax import lax
from jax.experimental import pallas as pl
from jax.experimental.pallas import tpu as pltpu
from jax.sharding import PartitionSpec as P

AXES = ("leaf", "near")
RANK = 64


def split_three(x):
    hi = x.astype(jnp.bfloat16)
    rest = x - hi.astype(jnp.float32)
    mid = rest.astype(jnp.bfloat16)
    return hi, mid, (rest - mid.astype(jnp.float32)).astype(jnp.bfloat16)


def dot32(a, b):
    return jnp.dot(a, b, preferred_element_type=jnp.float32)


def dot_last(a, b):
    return lax.dot_general(a, b, (((1,), (1,)), ((), ())), preferred_element_type=jnp.float32)


def congruence(gram, transfer):
    across = jnp.transpose(transfer.astype(jnp.float32)).astype(jnp.bfloat16)
    hi, mid, low = split_three(gram)
    half = dot32(hi, transfer) + (dot32(mid, transfer) + dot32(low, transfer))
    hi, mid, low = split_three(half)
    return dot32(across, hi) + (dot32(across, mid) + dot32(across, low))


def unit_matrix():
    rows = lax.broadcasted_iota(jnp.int32, (RANK, RANK), 0)
    cols = lax.broadcasted_iota(jnp.int32, (RANK, RANK), 1)
    return (rows == cols).astype(jnp.float32)


def factor_panels(matrices):
    shape = (8, RANK)
    work = [list(panels) for panels in matrices]
    rows = lax.broadcasted_iota(jnp.int32, shape, 0)
    cols = lax.broadcasted_iota(jnp.int32, shape, 1)
    factors = [[None] * 8 for _ in work]
    for step in range(8):
        base = 8 * step
        for panels, factor in zip(work, factors):
            panel = panels[step]
            column = [
                jnp.broadcast_to(panel[:, base + k : base + k + 1], shape) for k in range(8)
            ]
            weights = [
                [jnp.broadcast_to(lower[:, base + k : base + k + 1], shape) for k in range(8)]
                for lower in panels[step + 1 :]
            ]
            rows_out = jnp.zeros(shape, jnp.float32)
            for j in range(8):
                here = rows == j
                pivot = jnp.broadcast_to(column[j][j : j + 1, :], shape)
                panel_row = jnp.broadcast_to(panel[j : j + 1, :], shape)
                rows_out = jnp.where(here, panel_row * lax.rsqrt(pivot), rows_out)
                inverse = 1.0 / pivot
                scale = column[j] * inverse
                for k in range(j + 1, 8):
                    entry = jnp.broadcast_to(column[k][j : j + 1, :], shape)
                    column[k] = jnp.where(here, entry * inverse, column[k] - scale * entry)
                panel = jnp.where(here, panel_row * inverse, panel - scale * panel_row)
            factor[step] = jnp.where(cols >= rows + base, rows_out, 0.0)
            for at, weight in enumerate(weights):
                lower = panels[step + 1 + at]
                for k in range(8):
                    lower = lower - weight[k] * jnp.broadcast_to(panel[k : k + 1, :], shape)
                panels[step + 1 + at] = lower
    return factors


def in_vmem(x):
    return pltpu.with_memory_space_constraint(x, pltpu.VMEM)


def panels_of(matrix):
    return [matrix[8 * p : 8 * p + 8, :] for p in range(8)]


def store_panels(ref, n, panels):
    for p in range(8):
        ref[n, 8 * p : 8 * p + 8, :] = panels[p]


def factor_kernel(*refs):
    grams, factors = refs[:-1], refs[-1]
    matrices = []
    for gram in grams:
        if len(gram.shape) == 2:
            matrices.append(panels_of(gram[...]))
        else:
            matrices += [panels_of(gram[n]) for n in range(gram.shape[0])]
    for n, panels in enumerate(factor_panels(matrices)):
        store_panels(factors, n, panels)


def factor(*grams, keep=False):
    count = sum(1 if gram.ndim == 2 else gram.shape[0] for gram in grams)
    vmem = pl.BlockSpec(memory_space=pltpu.VMEM)
    kind = pltpu.VMEM if keep else jax.ShapeDtypeStruct
    return pl.pallas_call(
        factor_kernel,
        in_specs=[vmem] * len(grams),
        out_specs=vmem,
        out_shape=kind((count, RANK, RANK), jnp.float32),
        compiler_params=limit(4),
        name="factor",
    )(*[in_vmem(gram) for gram in grams])


def limit(mebibytes):
    return pltpu.CompilerParams(vmem_limit_bytes=mebibytes << 20)


RING = ((0, 1, 2), (1, 2, 0))


def ring_swap(x, stage, flip, devices):
    pairs = [(d, d ^ flip << 1 + 2 * RING[d & 1][stage]) for d in range(devices)]
    return lax.ppermute(x, AXES, pairs)


def grid_places(device):
    first = (device >> 1 & 1) + 2 * (device >> 4 & 1)
    second = (device >> 2 & 1) + 2 * (device >> 5 & 1)
    third = (device & 1) + 2 * (device >> 3 & 1) + 4 * (device >> 6 & 1)
    return first, second, third


def grid_device(first, second, third):
    low = (third & 1) + 2 * (first & 1) + 4 * (second & 1) + 8 * (third >> 1 & 1)
    return low + 16 * (first >> 1) + 32 * (second >> 1) + 64 * (third >> 2)


def grid_swap(x, dim, shift, devices):
    pairs = []
    for d in range(devices):
        place = list(grid_places(d))
        to = place[dim] + (1 if place[dim] % 2 == shift else -1)
        if 0 <= to < (4, 4, 8)[dim]:
            place[dim] = to
        pairs.append((d, grid_device(*place)))
    return lax.ppermute(x, AXES, pairs)


def neighbours(lower, upper, dim, odd, devices):
    even_pairs = grid_swap(jnp.where(odd, lower, upper), dim, 0, devices)
    odd_pairs = grid_swap(jnp.where(odd, upper, lower), dim, 1, devices)
    return jnp.where(odd, even_pairs, odd_pairs), jnp.where(odd, odd_pairs, even_pairs)


def swap_cores(x, devices):
    return lax.ppermute(x, AXES, [(d, d ^ 1) for d in range(devices)])


def exchange_vectors(own, device, devices):
    first, second, _ = grid_places(device)
    left, right = neighbours(own[0::2], own[1::2], 0, first % 2 == 1, devices)
    rows = jnp.stack([left, own[0::2], own[1::2], right], axis=1)
    before, after = neighbours(rows[0], rows[1], 1, second % 2 == 1, devices)
    plane = jnp.concatenate([before, rows[0], rows[1], after])
    return [plane, swap_cores(plane, devices), grid_swap(plane, 2, 1, devices)]


def vector_slots(near_index, device):
    first, second, third = grid_places(device)
    cell = near_index
    x = (cell & 1) + 2 * (cell >> 3 & 1) + 4 * (cell >> 6 & 1) - 2 * first
    y = (cell >> 1 & 1) + 2 * (cell >> 4 & 1) + 4 * (cell >> 7 & 1) - 2 * second
    z = (cell >> 2 & 1) + 2 * (cell >> 5 & 1) + 4 * (cell >> 8 & 1)
    plane = jnp.where(z == third, 0, jnp.where(z >> 1 == third >> 1, 1, 2))
    return 16 * plane + 4 * (y + 1) + x + 1


def gather_weights(own, devices):
    held = own
    for stage in range(2):
        for flip in (1, 3):
            held = jnp.concatenate([held, ring_swap(held, stage, flip, devices)])
    near = ring_swap(held, 2, 1, devices)
    last = ring_swap(held, 2, 3, devices)
    return [held, near, last]


def gather_far(near, last, devices):
    half = near.shape[0] // 2
    return [ring_swap(last[:half], 2, 1, devices), ring_swap(near[half:], 2, 3, devices)]


def weight_tiles(adm_index, device):
    owner = adm_index >> 2
    label = []
    for axis in range(3):
        apart = (owner ^ device) >> 1 + 2 * axis & 3
        label.append(apart ^ apart >> 1)
    order = [
        label[RING[0][2]] * 16 + label[RING[0][1]] * 4 + label[RING[0][0]],
        label[RING[1][2]] * 16 + label[RING[1][1]] * 4 + label[RING[1][0]],
    ]
    core = owner & 1
    other = core ^ (device & 1)
    return other * 128 + 2 * jnp.where(core == 1, order[1], order[0]) + (adm_index >> 1 & 1)


def join_pieces(pieces, buffer):
    at = 0
    for piece in pieces:
        buffer[at : at + piece.shape[0]] = piece[...]
        at += piece.shape[0]


def near_kernel(slots, blocks, samples, basis, *rest):
    pieces, (gram, vectors) = rest[:3], rest[3:]
    join_pieces(pieces, vectors)
    for leaf in range(blocks.shape[0]):
        near_leaf(leaf, slots, blocks, samples, basis, vectors, gram)


def near_leaf(leaf, slots, blocks, samples, basis, vectors, gram):
    total = None
    for k in range(8):
        part = dot_last(vectors[slots[8 * leaf + k]], blocks[leaf, k])
        total = part if total is None else total + part
    far = (samples[leaf].astype(jnp.float32) - total).astype(jnp.bfloat16)
    scale = RANK**-0.5
    wide = dot_last(basis[leaf], far) * scale
    tall = dot_last(far, basis[leaf]) * scale
    wide_hi = wide.astype(jnp.bfloat16)
    wide_low = (wide - wide_hi.astype(jnp.float32)).astype(jnp.bfloat16)
    tall_hi = tall.astype(jnp.bfloat16)
    tall_low = (tall - tall_hi.astype(jnp.float32)).astype(jnp.bfloat16)
    gram[leaf] = dot32(tall_hi, wide_hi) + (dot32(tall_hi, wide_low) + dot32(tall_low, wide_hi))


def near_grams(slots, near_blocks, samples, leaf_basis, pieces):
    count, rank, size = samples.shape
    vmem = pl.BlockSpec(memory_space=pltpu.VMEM)
    return pl.pallas_call(
        near_kernel,
        in_specs=[pl.BlockSpec(memory_space=pltpu.SMEM)] + [vmem] * (3 + len(pieces)),
        out_specs=vmem,
        out_shape=pltpu.VMEM((count, rank, rank), jnp.float32),
        scratch_shapes=[pltpu.VMEM((48, rank, size), jnp.bfloat16)],
        compiler_params=limit(8),
        name="near_grams",
    )(
        slots,
        in_vmem(near_blocks),
        in_vmem(samples),
        in_vmem(leaf_basis),
        *[in_vmem(piece) for piece in pieces],
    )


def select_kernel(nodes, upper_transfer, transfers, semaphores):
    copies = [
        pltpu.make_async_copy(upper_transfer.at[nodes[n]], transfers.at[n], semaphores.at[n])
        for n in range(transfers.shape[0])
    ]
    for copy in copies:
        copy.start()
    for copy in copies:
        copy.wait()


def select_transfers(nodes, upper_transfer):
    levels, rank = nodes.shape[0], upper_transfer.shape[1]
    return pl.pallas_call(
        select_kernel,
        in_specs=[
            pl.BlockSpec(memory_space=pltpu.SMEM),
            pl.BlockSpec(memory_space=pl.ANY),
        ],
        out_specs=pl.BlockSpec(memory_space=pltpu.VMEM),
        out_shape=pltpu.VMEM((levels, rank, rank), jnp.bfloat16),
        scratch_shapes=[pltpu.SemaphoreType.DMA((levels,))],
        compiler_params=limit(4),
        name="select_transfers",
    )(nodes, upper_transfer)


def leaf_kernel(tiles, halves, coupling, near_gram, leaf_transfer, inner_transfer, *rest):
    pieces, (leaf_grams, inner_grams, sent, weights, coupled) = rest[:10], rest[10:]
    join_pieces(pieces, weights)
    unit = unit_matrix()
    moved = []
    for leaf in range(leaf_grams.shape[0]):
        sums = coupled_gram(leaf, tiles, halves, coupling, weights, coupled.at[leaf % 2])
        gram = near_gram[leaf] + sums * (1.0 / 2048) + unit
        leaf_grams[leaf] = gram
        moved.append(congruence(gram, leaf_transfer[leaf]))
    first = 0.5 * (moved[0] + moved[1]) + unit
    second = 0.5 * (moved[2] + moved[3]) + unit
    inner_grams[0] = first
    inner_grams[1] = second
    top = congruence(first, inner_transfer[0, 0]) + congruence(second, inner_transfer[0, 1])
    top = 0.5 * top + unit
    inner_grams[2] = top
    sent[...] = congruence(top, inner_transfer[0, 2])


def coupled_gram(leaf, tiles, halves, coupling, weights, coupled):
    side = lax.broadcasted_iota(jnp.int32, (RANK, 2 * RANK), 1) >> 6
    nothing = jnp.zeros((RANK, 2 * RANK), jnp.bfloat16)
    for pair in range(16):
        chosen = []
        for s in (2 * pair, 2 * pair + 1):
            tile = weights[tiles[32 * leaf + s]]
            chosen.append(jnp.where(side == halves[32 * leaf + s], tile, nothing))
        both = jnp.concatenate(
            [
                jnp.concatenate([chosen[0], nothing], axis=1),
                jnp.concatenate([nothing, chosen[1]], axis=1),
            ],
            axis=0,
        )
        product = dot32(coupling[leaf, :, 128 * pair : 128 * pair + 128], both).astype(jnp.bfloat16)
        coupled[128 * pair : 128 * pair + 64, :] = product[:, :128]
        coupled[128 * pair + 64 : 128 * pair + 128, :] = product[:, 128:]
    square = lax.dot_general(
        coupled[...], coupled[...], (((0,), (0,)), ((), ())), preferred_element_type=jnp.float32
    )
    return square[:RANK, :RANK] + square[RANK:, RANK:]


def leaf_levels(tiles, halves, coupling, near_gram, leaf_transfer, inner_transfer, pieces):
    count, rank, width = coupling.shape
    vmem = pl.BlockSpec(memory_space=pltpu.VMEM)
    inputs = [coupling, near_gram, leaf_transfer, inner_transfer] + list(pieces)
    return pl.pallas_call(
        leaf_kernel,
        in_specs=[pl.BlockSpec(memory_space=pltpu.SMEM)] * 2 + [vmem] * len(inputs),
        out_specs=[vmem] * 3,
        out_shape=[
            pltpu.VMEM((count, rank, rank), jnp.float32),
            pltpu.VMEM((count - 1, rank, rank), jnp.float32),
            pltpu.VMEM((rank, rank), jnp.float32),
        ],
        scratch_shapes=[
            pltpu.VMEM((256, rank, 2 * rank), jnp.bfloat16),
            pltpu.VMEM((2, width, 2 * rank), jnp.bfloat16),
        ],
        compiler_params=limit(12),
        name="leaf_levels",
    )(tiles, halves, *[in_vmem(x) for x in inputs])


def merged(one, other):
    return 0.5 * (one + other) + unit_matrix()


def pair_kernel(own, other, transfers, gram, sent):
    here = merged(own[...], other[...])
    gram[...] = here
    sent[...] = congruence(here, transfers[0])


def merge_pair(own, other, transfers):
    vmem = pl.BlockSpec(memory_space=pltpu.VMEM)
    return pl.pallas_call(
        pair_kernel,
        in_specs=[vmem] * 3,
        out_specs=[vmem] * 2,
        out_shape=[pltpu.VMEM((RANK, RANK), jnp.float32)] * 2,
        compiler_params=limit(4),
        name="merge_pair",
    )(in_vmem(own), in_vmem(other), in_vmem(transfers))


def two_levels(own, others, transfers, at, beside):
    sibling, cousin, partner = others
    here = merged(own[...], sibling[...])
    there = merged(cousin[...], partner[...])
    above = merged(congruence(here, transfers[at]), congruence(there, transfers[beside]))
    return here, above


def quad_kernel(at, beside, own, *rest):
    others, transfers, (low, high, sent) = rest[:3], rest[3], rest[4:]
    here, above = two_levels(own, others, transfers, at, beside)
    low[...] = here
    high[...] = above
    sent[...] = congruence(above, transfers[at + 1])


def merge_quad(at, beside, own, others, transfers):
    vmem = pl.BlockSpec(memory_space=pltpu.VMEM)
    return pl.pallas_call(
        functools.partial(quad_kernel, at, beside),
        in_specs=[vmem] * 5,
        out_specs=[vmem] * 3,
        out_shape=[pltpu.VMEM((RANK, RANK), jnp.float32)] * 3,
        compiler_params=limit(4),
        name="merge_quad",
    )(in_vmem(own), *[in_vmem(x) for x in others], in_vmem(transfers))


def root_kernel(at, beside, own, *rest):
    others, transfers, done, factors = rest[:3], rest[3], rest[4], rest[5]
    pair = two_levels(own, others, transfers, at, beside)
    count = done.shape[0]
    for n, panels in enumerate(factor_panels([panels_of(gram) for gram in pair])):
        store_panels(factors, count + n, panels)
    for n in range(count):
        factors[n] = done[n]


def factor_root(at, beside, own, others, transfers, done):
    vmem = pl.BlockSpec(memory_space=pltpu.VMEM)
    return pl.pallas_call(
        functools.partial(root_kernel, at, beside),
        in_specs=[vmem] * 6,
        out_specs=vmem,
        out_shape=jax.ShapeDtypeStruct((done.shape[0] + 2, RANK, RANK), jnp.float32),
        compiler_params=limit(4),
        name="factor_root",
    )(in_vmem(own), *[in_vmem(x) for x in others], in_vmem(transfers), in_vmem(done))


def body(
    near_blocks,
    near_index,
    test_vectors,
    samples,
    leaf_basis,
    col_weights,
    coupling,
    adm_index,
    adm_count,
    leaf_transfer,
    inner_transfer,
    upper_transfer,
):
    count, rank, size = test_vectors.shape
    slots = adm_index.shape[1]
    devices = lax.axis_size("leaf") * lax.axis_size("near")
    total_levels = devices.bit_length() - 1
    device = lax.axis_index("leaf") * lax.axis_size("near") + lax.axis_index("near")
    paired = jnp.concatenate([col_weights[0::2], col_weights[1::2]], axis=2)
    weights = gather_weights(paired, devices)
    vectors = exchange_vectors(test_vectors, device, devices)
    levels = jnp.arange(1, total_levels)
    starts = devices - (devices >> levels - 1)
    nodes = jnp.concatenate(
        [starts + (device >> levels), starts[1::2] + (device >> levels[1::2] ^ 1)]
    )
    held, upper_transfer = lax.optimization_barrier((weights[0], upper_transfer))
    transfers = select_transfers(nodes, upper_transfer)
    live = jnp.arange(slots)[None, :] < adm_count[:, None]
    halves = jnp.where(live, adm_index & 1, 2).reshape(-1)
    tiles = weight_tiles(adm_index, device).reshape(-1)
    wanted = vector_slots(near_index, device).reshape(-1)
    near, last, transfers, halves, tiles, wanted = lax.optimization_barrier(
        (weights[1], weights[2], transfers, halves, tiles, wanted)
    )
    far = gather_far(near, last, devices)
    weights = [held, near, last]
    swapped = [swap_cores(piece, devices) for piece in weights]
    near_gram = near_grams(wanted, near_blocks, samples, leaf_basis, vectors)
    far_low, far_high, near_gram = lax.optimization_barrier((far[0], far[1], near_gram))
    far = [far_low, far_high]
    weights = weights + far + swapped + [swap_cores(piece, devices) for piece in far]
    gram, inner_grams, sent = leaf_levels(
        tiles,
        halves,
        coupling,
        near_gram,
        leaf_transfer,
        inner_transfer,
        weights,
    )
    def swapped_with(x, flip):
        return lax.ppermute(x, AXES, [(d, d ^ flip) for d in range(devices)])

    other = swapped_with(sent, 1)
    first, sent = merge_pair(sent, other, transfers)
    grams = [first]
    local = []
    for axis in range(3):
        own = sent
        others = [swapped_with(own, flip << 1 + 2 * axis) for flip in (1, 2, 3)]
        if axis == 0:
            ready = factor(gram)
        elif axis == 1:
            ready = factor(inner_grams)
        else:
            ready = factor(*grams, keep=True)
        others[1], ready = lax.optimization_barrier((others[1], ready))
        at = 1 + 2 * axis
        if axis < 2:
            local.append(ready)
            low, high, sent = merge_quad(at, total_levels - 1 + axis, own, others, transfers)
            grams += [low, high]
        else:
            upper_factors = factor_root(at, total_levels - 1 + axis, own, others, transfers, ready)
    return (local[0], local[1][None], upper_factors[None])


def solution(mesh):
    split = P(AXES)
    return jax.shard_map(
        body,
        mesh=mesh,
        in_specs=(split,) * 11 + (P(),),
        out_specs=(split,) * 3,
        check_vma=False,
    )
```

```python
import functools

import jax
import jax.numpy as jnp
from jax import lax
from jax.experimental import pallas as pl
from jax.experimental.pallas import tpu as pltpu
from jax.sharding import PartitionSpec as P

AXES = ("leaf", "near")
RANK = 64


def split_three(x):
    hi = x.astype(jnp.bfloat16)
    rest = x - hi.astype(jnp.float32)
    mid = rest.astype(jnp.bfloat16)
    return hi, mid, (rest - mid.astype(jnp.float32)).astype(jnp.bfloat16)


def dot32(a, b):
    return jnp.dot(a, b, preferred_element_type=jnp.float32)


def dot_last(a, b):
    return lax.dot_general(a, b, (((1,), (1,)), ((), ())), preferred_element_type=jnp.float32)


def congruence(gram, transfer):
    across = jnp.transpose(transfer.astype(jnp.float32)).astype(jnp.bfloat16)
    hi, mid, low = split_three(gram)
    half = dot32(hi, transfer) + (dot32(mid, transfer) + dot32(low, transfer))
    hi, mid, low = split_three(half)
    return dot32(across, hi) + (dot32(across, mid) + dot32(across, low))


def unit_matrix():
    rows = lax.broadcasted_iota(jnp.int32, (RANK, RANK), 0)
    cols = lax.broadcasted_iota(jnp.int32, (RANK, RANK), 1)
    return (rows == cols).astype(jnp.float32)


def factor_panels(matrices):
    shape = (8, RANK)
    work = [list(panels) for panels in matrices]
    rows = lax.broadcasted_iota(jnp.int32, shape, 0)
    cols = lax.broadcasted_iota(jnp.int32, shape, 1)
    factors = [[None] * 8 for _ in work]
    for step in range(8):
        base = 8 * step
        for panels, factor in zip(work, factors):
            panel = panels[step]
            column = [
                jnp.broadcast_to(panel[:, base + k : base + k + 1], shape) for k in range(8)
            ]
            weights = [
                [jnp.broadcast_to(lower[:, base + k : base + k + 1], shape) for k in range(8)]
                for lower in panels[step + 1 :]
            ]
            rows_out = jnp.zeros(shape, jnp.float32)
            for j in range(8):
                here = rows == j
                pivot = jnp.broadcast_to(column[j][j : j + 1, :], shape)
                panel_row = jnp.broadcast_to(panel[j : j + 1, :], shape)
                rows_out = jnp.where(here, panel_row * lax.rsqrt(pivot), rows_out)
                inverse = 1.0 / pivot
                scale = column[j] * inverse
                for k in range(j + 1, 8):
                    entry = jnp.broadcast_to(column[k][j : j + 1, :], shape)
                    column[k] = jnp.where(here, entry * inverse, column[k] - scale * entry)
                panel = jnp.where(here, panel_row * inverse, panel - scale * panel_row)
            factor[step] = jnp.where(cols >= rows + base, rows_out, 0.0)
            for at, weight in enumerate(weights):
                lower = panels[step + 1 + at]
                for k in range(8):
                    lower = lower - weight[k] * jnp.broadcast_to(panel[k : k + 1, :], shape)
                panels[step + 1 + at] = lower
    return factors


def in_vmem(x):
    return pltpu.with_memory_space_constraint(x, pltpu.VMEM)


def panels_of(matrix):
    return [matrix[8 * p : 8 * p + 8, :] for p in range(8)]


def store_panels(ref, n, panels):
    for p in range(8):
        ref[n, 8 * p : 8 * p + 8, :] = panels[p]


def factor_kernel(*refs):
    grams, factors = refs[:-1], refs[-1]
    matrices = []
    for gram in grams:
        if len(gram.shape) == 2:
            matrices.append(panels_of(gram[...]))
        else:
            matrices += [panels_of(gram[n]) for n in range(gram.shape[0])]
    for n, panels in enumerate(factor_panels(matrices)):
        store_panels(factors, n, panels)


def factor(*grams, keep=False):
    count = sum(1 if gram.ndim == 2 else gram.shape[0] for gram in grams)
    vmem = pl.BlockSpec(memory_space=pltpu.VMEM)
    kind = pltpu.VMEM if keep else jax.ShapeDtypeStruct
    return pl.pallas_call(
        factor_kernel,
        in_specs=[vmem] * len(grams),
        out_specs=vmem,
        out_shape=kind((count, RANK, RANK), jnp.float32),
        compiler_params=limit(4),
        name="factor",
    )(*[in_vmem(gram) for gram in grams])


def limit(mebibytes):
    return pltpu.CompilerParams(vmem_limit_bytes=mebibytes << 20)


RING = ((0, 1, 2), (1, 2, 0))


def ring_swap(x, stage, flip, devices):
    pairs = [(d, d ^ flip << 1 + 2 * RING[d & 1][stage]) for d in range(devices)]
    return lax.ppermute(x, AXES, pairs)


def grid_places(device):
    first = (device >> 1 & 1) + 2 * (device >> 4 & 1)
    second = (device >> 2 & 1) + 2 * (device >> 5 & 1)
    third = (device & 1) + 2 * (device >> 3 & 1) + 4 * (device >> 6 & 1)
    return first, second, third


def grid_device(first, second, third):
    low = (third & 1) + 2 * (first & 1) + 4 * (second & 1) + 8 * (third >> 1 & 1)
    return low + 16 * (first >> 1) + 32 * (second >> 1) + 64 * (third >> 2)


def grid_swap(x, dim, shift, devices):
    pairs = []
    for d in range(devices):
        place = list(grid_places(d))
        to = place[dim] + (1 if place[dim] % 2 == shift else -1)
        if 0 <= to < (4, 4, 8)[dim]:
            place[dim] = to
        pairs.append((d, grid_device(*place)))
    return lax.ppermute(x, AXES, pairs)


def neighbours(lower, upper, dim, odd, devices):
    even_pairs = grid_swap(jnp.where(odd, lower, upper), dim, 0, devices)
    odd_pairs = grid_swap(jnp.where(odd, upper, lower), dim, 1, devices)
    return jnp.where(odd, even_pairs, odd_pairs), jnp.where(odd, odd_pairs, even_pairs)


def swap_cores(x, devices):
    return lax.ppermute(x, AXES, [(d, d ^ 1) for d in range(devices)])


def exchange_vectors(own, device, devices):
    first, second, _ = grid_places(device)
    left, right = neighbours(own[0::2], own[1::2], 0, first % 2 == 1, devices)
    rows = jnp.stack([left, own[0::2], own[1::2], right], axis=1)
    before, after = neighbours(rows[0], rows[1], 1, second % 2 == 1, devices)
    plane = jnp.concatenate([before, rows[0], rows[1], after])
    return [plane, swap_cores(plane, devices), grid_swap(plane, 2, 1, devices)]


def vector_slots(near_index, device):
    first, second, third = grid_places(device)
    cell = near_index
    x = (cell & 1) + 2 * (cell >> 3 & 1) + 4 * (cell >> 6 & 1) - 2 * first
    y = (cell >> 1 & 1) + 2 * (cell >> 4 & 1) + 4 * (cell >> 7 & 1) - 2 * second
    z = (cell >> 2 & 1) + 2 * (cell >> 5 & 1) + 4 * (cell >> 8 & 1)
    plane = jnp.where(z == third, 0, jnp.where(z >> 1 == third >> 1, 1, 2))
    return 16 * plane + 4 * (y + 1) + x + 1


def gather_weights(own, devices):
    held = own
    for stage in range(2):
        others = [ring_swap(held, stage, flip, devices) for flip in (1, 3, 2)]
        held = jnp.concatenate([held] + others)
    near = ring_swap(held, 2, 1, devices)
    last = ring_swap(held, 2, 3, devices)
    return [held, near, last]


def gather_far(near, last, devices):
    half = near.shape[0] // 2
    return [ring_swap(last[:half], 2, 1, devices), ring_swap(near[half:], 2, 3, devices)]


def weight_tiles(adm_index, device):
    owner = adm_index >> 2
    label = []
    for axis in range(3):
        apart = (owner ^ device) >> 1 + 2 * axis & 3
        label.append(apart ^ apart >> 1)
    order = [
        label[RING[0][2]] * 16 + label[RING[0][1]] * 4 + label[RING[0][0]],
        label[RING[1][2]] * 16 + label[RING[1][1]] * 4 + label[RING[1][0]],
    ]
    core = owner & 1
    other = core ^ (device & 1)
    return other * 128 + 2 * jnp.where(core == 1, order[1], order[0]) + (adm_index >> 1 & 1)


def join_pieces(pieces, buffer):
    at = 0
    for piece in pieces:
        buffer[at : at + piece.shape[0]] = piece[...]
        at += piece.shape[0]


def near_kernel(slots, blocks, samples, basis, *rest):
    pieces, (gram, vectors) = rest[:3], rest[3:]
    join_pieces(pieces, vectors)
    for leaf in range(blocks.shape[0]):
        near_leaf(leaf, slots, blocks, samples, basis, vectors, gram)


def near_leaf(leaf, slots, blocks, samples, basis, vectors, gram):
    total = None
    for k in range(8):
        part = dot_last(vectors[slots[8 * leaf + k]], blocks[leaf, k])
        total = part if total is None else total + part
    far = (samples[leaf].astype(jnp.float32) - total).astype(jnp.bfloat16)
    scale = RANK**-0.5
    wide = dot_last(basis[leaf], far) * scale
    tall = dot_last(far, basis[leaf]) * scale
    wide_hi = wide.astype(jnp.bfloat16)
    wide_low = (wide - wide_hi.astype(jnp.float32)).astype(jnp.bfloat16)
    tall_hi = tall.astype(jnp.bfloat16)
    tall_low = (tall - tall_hi.astype(jnp.float32)).astype(jnp.bfloat16)
    gram[leaf] = dot32(tall_hi, wide_hi) + (dot32(tall_hi, wide_low) + dot32(tall_low, wide_hi))


def near_grams(slots, near_blocks, samples, leaf_basis, pieces):
    count, rank, size = samples.shape
    vmem = pl.BlockSpec(memory_space=pltpu.VMEM)
    return pl.pallas_call(
        near_kernel,
        in_specs=[pl.BlockSpec(memory_space=pltpu.SMEM)] + [vmem] * (3 + len(pieces)),
        out_specs=vmem,
        out_shape=pltpu.VMEM((count, rank, rank), jnp.float32),
        scratch_shapes=[pltpu.VMEM((48, rank, size), jnp.bfloat16)],
        compiler_params=limit(8),
        name="near_grams",
    )(
        slots,
        in_vmem(near_blocks),
        in_vmem(samples),
        in_vmem(leaf_basis),
        *[in_vmem(piece) for piece in pieces],
    )


def select_kernel(nodes, upper_transfer, transfers, semaphores):
    copies = [
        pltpu.make_async_copy(upper_transfer.at[nodes[n]], transfers.at[n], semaphores.at[n])
        for n in range(transfers.shape[0])
    ]
    for copy in copies:
        copy.start()
    for copy in copies:
        copy.wait()


def select_transfers(nodes, upper_transfer):
    levels, rank = nodes.shape[0], upper_transfer.shape[1]
    return pl.pallas_call(
        select_kernel,
        in_specs=[
            pl.BlockSpec(memory_space=pltpu.SMEM),
            pl.BlockSpec(memory_space=pl.ANY),
        ],
        out_specs=pl.BlockSpec(memory_space=pltpu.VMEM),
        out_shape=pltpu.VMEM((levels, rank, rank), jnp.bfloat16),
        scratch_shapes=[pltpu.SemaphoreType.DMA((levels,))],
        compiler_params=limit(4),
        name="select_transfers",
    )(nodes, upper_transfer)


def leaf_kernel(tiles, halves, coupling, near_gram, leaf_transfer, inner_transfer, *rest):
    pieces, (leaf_grams, inner_grams, sent, weights, coupled) = rest[:10], rest[10:]
    join_pieces(pieces, weights)
    unit = unit_matrix()
    moved = []
    for leaf in range(leaf_grams.shape[0]):
        sums = coupled_gram(leaf, tiles, halves, coupling, weights, coupled.at[leaf % 2])
        gram = near_gram[leaf] + sums * (1.0 / 2048) + unit
        leaf_grams[leaf] = gram
        moved.append(congruence(gram, leaf_transfer[leaf]))
    first = 0.5 * (moved[0] + moved[1]) + unit
    second = 0.5 * (moved[2] + moved[3]) + unit
    inner_grams[0] = first
    inner_grams[1] = second
    top = congruence(first, inner_transfer[0, 0]) + congruence(second, inner_transfer[0, 1])
    top = 0.5 * top + unit
    inner_grams[2] = top
    sent[...] = congruence(top, inner_transfer[0, 2])


def coupled_gram(leaf, tiles, halves, coupling, weights, coupled):
    side = lax.broadcasted_iota(jnp.int32, (RANK, 2 * RANK), 1) >> 6
    nothing = jnp.zeros((RANK, 2 * RANK), jnp.bfloat16)
    for pair in range(16):
        chosen = []
        for s in (2 * pair, 2 * pair + 1):
            tile = weights[tiles[32 * leaf + s]]
            chosen.append(jnp.where(side == halves[32 * leaf + s], tile, nothing))
        both = jnp.concatenate(
            [
                jnp.concatenate([chosen[0], nothing], axis=1),
                jnp.concatenate([nothing, chosen[1]], axis=1),
            ],
            axis=0,
        )
        product = dot32(coupling[leaf, :, 128 * pair : 128 * pair + 128], both).astype(jnp.bfloat16)
        coupled[128 * pair : 128 * pair + 64, :] = product[:, :128]
        coupled[128 * pair + 64 : 128 * pair + 128, :] = product[:, 128:]
    square = lax.dot_general(
        coupled[...], coupled[...], (((0,), (0,)), ((), ())), preferred_element_type=jnp.float32
    )
    return square[:RANK, :RANK] + square[RANK:, RANK:]


def leaf_levels(tiles, halves, coupling, near_gram, leaf_transfer, inner_transfer, pieces):
    count, rank, width = coupling.shape
    vmem = pl.BlockSpec(memory_space=pltpu.VMEM)
    inputs = [coupling, near_gram, leaf_transfer, inner_transfer] + list(pieces)
    return pl.pallas_call(
        leaf_kernel,
        in_specs=[pl.BlockSpec(memory_space=pltpu.SMEM)] * 2 + [vmem] * len(inputs),
        out_specs=[vmem] * 3,
        out_shape=[
            pltpu.VMEM((count, rank, rank), jnp.float32),
            pltpu.VMEM((count - 1, rank, rank), jnp.float32),
            pltpu.VMEM((rank, rank), jnp.float32),
        ],
        scratch_shapes=[
            pltpu.VMEM((256, rank, 2 * rank), jnp.bfloat16),
            pltpu.VMEM((2, width, 2 * rank), jnp.bfloat16),
        ],
        compiler_params=limit(12),
        name="leaf_levels",
    )(tiles, halves, *[in_vmem(x) for x in inputs])


def merged(one, other):
    return 0.5 * (one + other) + unit_matrix()


def pair_kernel(own, other, transfers, gram, sent):
    here = merged(own[...], other[...])
    gram[...] = here
    sent[...] = congruence(here, transfers[0])


def merge_pair(own, other, transfers):
    vmem = pl.BlockSpec(memory_space=pltpu.VMEM)
    return pl.pallas_call(
        pair_kernel,
        in_specs=[vmem] * 3,
        out_specs=[vmem] * 2,
        out_shape=[pltpu.VMEM((RANK, RANK), jnp.float32)] * 2,
        compiler_params=limit(4),
        name="merge_pair",
    )(in_vmem(own), in_vmem(other), in_vmem(transfers))


def two_levels(own, others, transfers, at, beside):
    sibling, cousin, partner = others
    here = merged(own[...], sibling[...])
    there = merged(cousin[...], partner[...])
    above = merged(congruence(here, transfers[at]), congruence(there, transfers[beside]))
    return here, above


def quad_kernel(at, beside, own, *rest):
    others, transfers, (low, high, sent) = rest[:3], rest[3], rest[4:]
    here, above = two_levels(own, others, transfers, at, beside)
    low[...] = here
    high[...] = above
    sent[...] = congruence(above, transfers[at + 1])


def merge_quad(at, beside, own, others, transfers):
    vmem = pl.BlockSpec(memory_space=pltpu.VMEM)
    return pl.pallas_call(
        functools.partial(quad_kernel, at, beside),
        in_specs=[vmem] * 5,
        out_specs=[vmem] * 3,
        out_shape=[pltpu.VMEM((RANK, RANK), jnp.float32)] * 3,
        compiler_params=limit(4),
        name="merge_quad",
    )(in_vmem(own), *[in_vmem(x) for x in others], in_vmem(transfers))


def root_kernel(at, beside, own, *rest):
    others, transfers, done, factors = rest[:3], rest[3], rest[4], rest[5]
    pair = two_levels(own, others, transfers, at, beside)
    count = done.shape[0]
    for n, panels in enumerate(factor_panels([panels_of(gram) for gram in pair])):
        store_panels(factors, count + n, panels)
    for n in range(count):
        factors[n] = done[n]


def factor_root(at, beside, own, others, transfers, done):
    vmem = pl.BlockSpec(memory_space=pltpu.VMEM)
    return pl.pallas_call(
        functools.partial(root_kernel, at, beside),
        in_specs=[vmem] * 6,
        out_specs=vmem,
        out_shape=jax.ShapeDtypeStruct((done.shape[0] + 2, RANK, RANK), jnp.float32),
        compiler_params=limit(4),
        name="factor_root",
    )(in_vmem(own), *[in_vmem(x) for x in others], in_vmem(transfers), in_vmem(done))


def body(
    near_blocks,
    near_index,
    test_vectors,
    samples,
    leaf_basis,
    col_weights,
    coupling,
    adm_index,
    adm_count,
    leaf_transfer,
    inner_transfer,
    upper_transfer,
):
    count, rank, size = test_vectors.shape
    slots = adm_index.shape[1]
    devices = lax.axis_size("leaf") * lax.axis_size("near")
    total_levels = devices.bit_length() - 1
    device = lax.axis_index("leaf") * lax.axis_size("near") + lax.axis_index("near")
    paired = jnp.concatenate([col_weights[0::2], col_weights[1::2]], axis=2)
    weights = gather_weights(paired, devices)
    vectors = exchange_vectors(test_vectors, device, devices)
    levels = jnp.arange(1, total_levels)
    starts = devices - (devices >> levels - 1)
    nodes = jnp.concatenate(
        [starts + (device >> levels), starts[1::2] + (device >> levels[1::2] ^ 1)]
    )
    held, upper_transfer = lax.optimization_barrier((weights[0], upper_transfer))
    transfers = select_transfers(nodes, upper_transfer)
    live = jnp.arange(slots)[None, :] < adm_count[:, None]
    halves = jnp.where(live, adm_index & 1, 2).reshape(-1)
    tiles = weight_tiles(adm_index, device).reshape(-1)
    wanted = vector_slots(near_index, device).reshape(-1)
    near, last, transfers, halves, tiles, wanted = lax.optimization_barrier(
        (weights[1], weights[2], transfers, halves, tiles, wanted)
    )
    far = gather_far(near, last, devices)
    weights = [held, near, last]
    swapped = [swap_cores(piece, devices) for piece in weights]
    near_gram = near_grams(wanted, near_blocks, samples, leaf_basis, vectors)
    far_low, far_high, near_gram = lax.optimization_barrier((far[0], far[1], near_gram))
    far = [far_low, far_high]
    weights = weights + far + swapped + [swap_cores(piece, devices) for piece in far]
    gram, inner_grams, sent = leaf_levels(
        tiles,
        halves,
        coupling,
        near_gram,
        leaf_transfer,
        inner_transfer,
        weights,
    )
    def swapped_with(x, flip):
        return lax.ppermute(x, AXES, [(d, d ^ flip) for d in range(devices)])

    other = swapped_with(sent, 1)
    first, sent = merge_pair(sent, other, transfers)
    grams = [first]
    local = []
    for axis in range(3):
        own = sent
        others = [swapped_with(own, flip << 1 + 2 * axis) for flip in (1, 2, 3)]
        if axis == 0:
            ready = factor(gram)
        elif axis == 1:
            ready = factor(inner_grams)
        else:
            ready = factor(*grams, keep=True)
        others[1], ready = lax.optimization_barrier((others[1], ready))
        at = 1 + 2 * axis
        if axis < 2:
            local.append(ready)
            low, high, sent = merge_quad(at, total_levels - 1 + axis, own, others, transfers)
            grams += [low, high]
        else:
            upper_factors = factor_root(at, total_levels - 1 + axis, own, others, transfers, ready)
    return (local[0], local[1][None], upper_factors[None])


def solution(mesh):
    split = P(AXES)
    return jax.shard_map(
        body,
        mesh=mesh,
        in_specs=(split,) * 11 + (P(),),
        out_specs=(split,) * 3,
        check_vma=False,
    )
```

```python
import functools

import jax
import jax.numpy as jnp
from jax import lax
from jax.experimental import pallas as pl
from jax.experimental.pallas import tpu as pltpu
from jax.sharding import PartitionSpec as P

AXES = ("leaf", "near")
RANK = 64


def split_three(x):
    hi = x.astype(jnp.bfloat16)
    rest = x - hi.astype(jnp.float32)
    mid = rest.astype(jnp.bfloat16)
    return hi, mid, (rest - mid.astype(jnp.float32)).astype(jnp.bfloat16)


def dot32(a, b):
    return jnp.dot(a, b, preferred_element_type=jnp.float32)


def dot_last(a, b):
    return lax.dot_general(a, b, (((1,), (1,)), ((), ())), preferred_element_type=jnp.float32)


def congruence(gram, transfer):
    across = jnp.transpose(transfer.astype(jnp.float32)).astype(jnp.bfloat16)
    hi, mid, low = split_three(gram)
    half = dot32(hi, transfer) + (dot32(mid, transfer) + dot32(low, transfer))
    hi, mid, low = split_three(half)
    return dot32(across, hi) + (dot32(across, mid) + dot32(across, low))


def unit_matrix():
    rows = lax.broadcasted_iota(jnp.int32, (RANK, RANK), 0)
    cols = lax.broadcasted_iota(jnp.int32, (RANK, RANK), 1)
    return (rows == cols).astype(jnp.float32)


def factor_panels(matrices):
    shape = (8, RANK)
    work = [list(panels) for panels in matrices]
    rows = lax.broadcasted_iota(jnp.int32, shape, 0)
    cols = lax.broadcasted_iota(jnp.int32, shape, 1)
    factors = [[None] * 8 for _ in work]
    for step in range(8):
        base = 8 * step
        for panels, factor in zip(work, factors):
            panel = panels[step]
            column = [
                jnp.broadcast_to(panel[:, base + k : base + k + 1], shape) for k in range(8)
            ]
            weights = [
                [jnp.broadcast_to(lower[:, base + k : base + k + 1], shape) for k in range(8)]
                for lower in panels[step + 1 :]
            ]
            rows_out = jnp.zeros(shape, jnp.float32)
            for j in range(8):
                here = rows == j
                pivot = jnp.broadcast_to(column[j][j : j + 1, :], shape)
                panel_row = jnp.broadcast_to(panel[j : j + 1, :], shape)
                rows_out = jnp.where(here, panel_row * lax.rsqrt(pivot), rows_out)
                inverse = 1.0 / pivot
                scale = column[j] * inverse
                for k in range(j + 1, 8):
                    entry = jnp.broadcast_to(column[k][j : j + 1, :], shape)
                    column[k] = jnp.where(here, entry * inverse, column[k] - scale * entry)
                panel = jnp.where(here, panel_row * inverse, panel - scale * panel_row)
            factor[step] = jnp.where(cols >= rows + base, rows_out, 0.0)
            for at, weight in enumerate(weights):
                lower = panels[step + 1 + at]
                for k in range(8):
                    lower = lower - weight[k] * jnp.broadcast_to(panel[k : k + 1, :], shape)
                panels[step + 1 + at] = lower
    return factors


def in_vmem(x):
    return pltpu.with_memory_space_constraint(x, pltpu.VMEM)


def panels_of(matrix):
    return [matrix[8 * p : 8 * p + 8, :] for p in range(8)]


def store_panels(ref, n, panels):
    for p in range(8):
        ref[n, 8 * p : 8 * p + 8, :] = panels[p]


def factor_kernel(*refs):
    grams, factors = refs[:-1], refs[-1]
    matrices = []
    for gram in grams:
        if len(gram.shape) == 2:
            matrices.append(panels_of(gram[...]))
        else:
            matrices += [panels_of(gram[n]) for n in range(gram.shape[0])]
    for n, panels in enumerate(factor_panels(matrices)):
        store_panels(factors, n, panels)


def factor(*grams, keep=False):
    count = sum(1 if gram.ndim == 2 else gram.shape[0] for gram in grams)
    vmem = pl.BlockSpec(memory_space=pltpu.VMEM)
    kind = pltpu.VMEM if keep else jax.ShapeDtypeStruct
    return pl.pallas_call(
        factor_kernel,
        in_specs=[vmem] * len(grams),
        out_specs=vmem,
        out_shape=kind((count, RANK, RANK), jnp.float32),
        compiler_params=limit(4),
        name="factor",
    )(*[in_vmem(gram) for gram in grams])


def limit(mebibytes):
    return pltpu.CompilerParams(vmem_limit_bytes=mebibytes << 20)


RING = ((0, 1, 2), (1, 2, 0))


def join_pieces(pieces, buffer):
    at = 0
    for piece in pieces:
        buffer[at : at + piece.shape[0]] = piece[...]
        at += piece.shape[0]


def join_kernel(*refs):
    join_pieces(refs[:-1], refs[-1])


def join(pieces):
    vmem = pl.BlockSpec(memory_space=pltpu.VMEM)
    shape = (sum(piece.shape[0] for piece in pieces),) + pieces[0].shape[1:]
    return pl.pallas_call(
        join_kernel,
        in_specs=[vmem] * len(pieces),
        out_specs=vmem,
        out_shape=pltpu.VMEM(shape, pieces[0].dtype),
        compiler_params=limit(4),
        name="join",
    )(*[in_vmem(piece) for piece in pieces])


def part_kernel(start, whole, part):
    part[...] = whole[start : start + part.shape[0]]


def part_of(whole, start, size):
    vmem = pl.BlockSpec(memory_space=pltpu.VMEM)
    return pl.pallas_call(
        functools.partial(part_kernel, start),
        in_specs=[vmem],
        out_specs=vmem,
        out_shape=pltpu.VMEM((size,) + whole.shape[1:], whole.dtype),
        compiler_params=limit(4),
        name="part",
    )(in_vmem(whole))


def ring_swap(x, stage, flip, devices):
    pairs = [(d, d ^ flip << 1 + 2 * RING[d & 1][stage]) for d in range(devices)]
    return lax.ppermute(x, AXES, pairs)


def grid_places(device):
    first = (device >> 1 & 1) + 2 * (device >> 4 & 1)
    second = (device >> 2 & 1) + 2 * (device >> 5 & 1)
    third = (device & 1) + 2 * (device >> 3 & 1) + 4 * (device >> 6 & 1)
    return first, second, third


def grid_device(first, second, third):
    low = (third & 1) + 2 * (first & 1) + 4 * (second & 1) + 8 * (third >> 1 & 1)
    return low + 16 * (first >> 1) + 32 * (second >> 1) + 64 * (third >> 2)


def grid_swap(x, dim, shift, devices):
    pairs = []
    for d in range(devices):
        place = list(grid_places(d))
        to = place[dim] + (1 if place[dim] % 2 == shift else -1)
        if 0 <= to < (4, 4, 8)[dim]:
            place[dim] = to
        pairs.append((d, grid_device(*place)))
    return lax.ppermute(x, AXES, pairs)


def neighbours(lower, upper, dim, odd, devices):
    even_pairs = grid_swap(jnp.where(odd, lower, upper), dim, 0, devices)
    odd_pairs = grid_swap(jnp.where(odd, upper, lower), dim, 1, devices)
    return jnp.where(odd, even_pairs, odd_pairs), jnp.where(odd, odd_pairs, even_pairs)


def swap_cores(x, devices):
    return lax.ppermute(x, AXES, [(d, d ^ 1) for d in range(devices)])


def exchange_vectors(own, device, devices):
    first, second, _ = grid_places(device)
    left, right = neighbours(own[0::2], own[1::2], 0, first % 2 == 1, devices)
    rows = jnp.stack([left, own[0::2], own[1::2], right], axis=1)
    before, after = neighbours(rows[0], rows[1], 1, second % 2 == 1, devices)
    plane = jnp.concatenate([before, rows[0], rows[1], after])
    return [plane, swap_cores(plane, devices), grid_swap(plane, 2, 1, devices)]


def vector_slots(near_index, device):
    first, second, third = grid_places(device)
    cell = near_index
    x = (cell & 1) + 2 * (cell >> 3 & 1) + 4 * (cell >> 6 & 1) - 2 * first
    y = (cell >> 1 & 1) + 2 * (cell >> 4 & 1) + 4 * (cell >> 7 & 1) - 2 * second
    z = (cell >> 2 & 1) + 2 * (cell >> 5 & 1) + 4 * (cell >> 8 & 1)
    plane = jnp.where(z == third, 0, jnp.where(z >> 1 == third >> 1, 1, 2))
    return 16 * plane + 4 * (y + 1) + x + 1


def gather_weights(own, devices):
    held = own
    for stage in range(2):
        others = [ring_swap(held, stage, flip, devices) for flip in (1, 3, 2)]
        held = join([held] + others)
    near = ring_swap(held, 2, 1, devices)
    last = ring_swap(held, 2, 3, devices)
    return [held, near, last]


def gather_far(near, last, devices):
    half = near.shape[0] // 2
    low, high = part_of(last, 0, half), part_of(near, half, half)
    return [ring_swap(low, 2, 1, devices), ring_swap(high, 2, 3, devices)]


def weight_tiles(adm_index, device):
    owner = adm_index >> 2
    label = []
    for axis in range(3):
        apart = (owner ^ device) >> 1 + 2 * axis & 3
        label.append(apart ^ apart >> 1)
    order = [
        label[RING[0][2]] * 16 + label[RING[0][1]] * 4 + label[RING[0][0]],
        label[RING[1][2]] * 16 + label[RING[1][1]] * 4 + label[RING[1][0]],
    ]
    core = owner & 1
    other = core ^ (device & 1)
    return other * 128 + 2 * jnp.where(core == 1, order[1], order[0]) + (adm_index >> 1 & 1)


def near_kernel(slots, blocks, samples, basis, *rest):
    pieces, (gram, vectors) = rest[:3], rest[3:]
    join_pieces(pieces, vectors)
    for leaf in range(blocks.shape[0]):
        near_leaf(leaf, slots, blocks, samples, basis, vectors, gram)


def near_leaf(leaf, slots, blocks, samples, basis, vectors, gram):
    total = None
    for k in range(8):
        part = dot_last(vectors[slots[8 * leaf + k]], blocks[leaf, k])
        total = part if total is None else total + part
    far = (samples[leaf].astype(jnp.float32) - total).astype(jnp.bfloat16)
    scale = RANK**-0.5
    wide = dot_last(basis[leaf], far) * scale
    tall = dot_last(far, basis[leaf]) * scale
    wide_hi = wide.astype(jnp.bfloat16)
    wide_low = (wide - wide_hi.astype(jnp.float32)).astype(jnp.bfloat16)
    tall_hi = tall.astype(jnp.bfloat16)
    tall_low = (tall - tall_hi.astype(jnp.float32)).astype(jnp.bfloat16)
    gram[leaf] = dot32(tall_hi, wide_hi) + (dot32(tall_hi, wide_low) + dot32(tall_low, wide_hi))


def near_grams(slots, near_blocks, samples, leaf_basis, pieces):
    count, rank, size = samples.shape
    vmem = pl.BlockSpec(memory_space=pltpu.VMEM)
    return pl.pallas_call(
        near_kernel,
        in_specs=[pl.BlockSpec(memory_space=pltpu.SMEM)] + [vmem] * (3 + len(pieces)),
        out_specs=vmem,
        out_shape=pltpu.VMEM((count, rank, rank), jnp.float32),
        scratch_shapes=[pltpu.VMEM((48, rank, size), jnp.bfloat16)],
        compiler_params=limit(8),
        name="near_grams",
    )(
        slots,
        in_vmem(near_blocks),
        in_vmem(samples),
        in_vmem(leaf_basis),
        *[in_vmem(piece) for piece in pieces],
    )


def select_kernel(nodes, upper_transfer, transfers, semaphores):
    copies = [
        pltpu.make_async_copy(upper_transfer.at[nodes[n]], transfers.at[n], semaphores.at[n])
        for n in range(transfers.shape[0])
    ]
    for copy in copies:
        copy.start()
    for copy in copies:
        copy.wait()


def select_transfers(nodes, upper_transfer):
    levels, rank = nodes.shape[0], upper_transfer.shape[1]
    return pl.pallas_call(
        select_kernel,
        in_specs=[
            pl.BlockSpec(memory_space=pltpu.SMEM),
            pl.BlockSpec(memory_space=pl.ANY),
        ],
        out_specs=pl.BlockSpec(memory_space=pltpu.VMEM),
        out_shape=pltpu.VMEM((levels, rank, rank), jnp.bfloat16),
        scratch_shapes=[pltpu.SemaphoreType.DMA((levels,))],
        compiler_params=limit(4),
        name="select_transfers",
    )(nodes, upper_transfer)


def leaf_kernel(tiles, halves, coupling, near_gram, leaf_transfer, inner_transfer, *rest):
    pieces, (leaf_grams, inner_grams, sent, weights, coupled) = rest[:10], rest[10:]
    join_pieces(pieces, weights)
    unit = unit_matrix()
    moved = []
    for leaf in range(leaf_grams.shape[0]):
        sums = coupled_gram(leaf, tiles, halves, coupling, weights, coupled.at[leaf % 2])
        gram = near_gram[leaf] + sums * (1.0 / 2048) + unit
        leaf_grams[leaf] = gram
        moved.append(congruence(gram, leaf_transfer[leaf]))
    first = 0.5 * (moved[0] + moved[1]) + unit
    second = 0.5 * (moved[2] + moved[3]) + unit
    inner_grams[0] = first
    inner_grams[1] = second
    top = congruence(first, inner_transfer[0, 0]) + congruence(second, inner_transfer[0, 1])
    top = 0.5 * top + unit
    inner_grams[2] = top
    sent[...] = congruence(top, inner_transfer[0, 2])


def coupled_gram(leaf, tiles, halves, coupling, weights, coupled):
    side = lax.broadcasted_iota(jnp.int32, (RANK, 2 * RANK), 1) >> 6
    nothing = jnp.zeros((RANK, 2 * RANK), jnp.bfloat16)
    for pair in range(16):
        chosen = []
        for s in (2 * pair, 2 * pair + 1):
            tile = weights[tiles[32 * leaf + s]]
            chosen.append(jnp.where(side == halves[32 * leaf + s], tile, nothing))
        both = jnp.concatenate(
            [
                jnp.concatenate([chosen[0], nothing], axis=1),
                jnp.concatenate([nothing, chosen[1]], axis=1),
            ],
            axis=0,
        )
        product = dot32(coupling[leaf, :, 128 * pair : 128 * pair + 128], both).astype(jnp.bfloat16)
        coupled[128 * pair : 128 * pair + 64, :] = product[:, :128]
        coupled[128 * pair + 64 : 128 * pair + 128, :] = product[:, 128:]
    square = lax.dot_general(
        coupled[...], coupled[...], (((0,), (0,)), ((), ())), preferred_element_type=jnp.float32
    )
    return square[:RANK, :RANK] + square[RANK:, RANK:]


def leaf_levels(tiles, halves, coupling, near_gram, leaf_transfer, inner_transfer, pieces):
    count, rank, width = coupling.shape
    vmem = pl.BlockSpec(memory_space=pltpu.VMEM)
    inputs = [coupling, near_gram, leaf_transfer, inner_transfer] + list(pieces)
    return pl.pallas_call(
        leaf_kernel,
        in_specs=[pl.BlockSpec(memory_space=pltpu.SMEM)] * 2 + [vmem] * len(inputs),
        out_specs=[vmem] * 3,
        out_shape=[
            pltpu.VMEM((count, rank, rank), jnp.float32),
            pltpu.VMEM((count - 1, rank, rank), jnp.float32),
            pltpu.VMEM((rank, rank), jnp.float32),
        ],
        scratch_shapes=[
            pltpu.VMEM((256, rank, 2 * rank), jnp.bfloat16),
            pltpu.VMEM((2, width, 2 * rank), jnp.bfloat16),
        ],
        compiler_params=limit(12),
        name="leaf_levels",
    )(tiles, halves, *[in_vmem(x) for x in inputs])


def merged(one, other):
    return 0.5 * (one + other) + unit_matrix()


def pair_kernel(own, other, transfers, gram, sent):
    here = merged(own[...], other[...])
    gram[...] = here
    sent[...] = congruence(here, transfers[0])


def merge_pair(own, other, transfers):
    vmem = pl.BlockSpec(memory_space=pltpu.VMEM)
    return pl.pallas_call(
        pair_kernel,
        in_specs=[vmem] * 3,
        out_specs=[vmem] * 2,
        out_shape=[pltpu.VMEM((RANK, RANK), jnp.float32)] * 2,
        compiler_params=limit(4),
        name="merge_pair",
    )(in_vmem(own), in_vmem(other), in_vmem(transfers))


def two_levels(own, others, transfers, at, beside):
    sibling, cousin, partner = others
    here = merged(own[...], sibling[...])
    there = merged(cousin[...], partner[...])
    above = merged(congruence(here, transfers[at]), congruence(there, transfers[beside]))
    return here, above


def quad_kernel(at, beside, own, *rest):
    others, transfers, (low, high, sent) = rest[:3], rest[3], rest[4:]
    here, above = two_levels(own, others, transfers, at, beside)
    low[...] = here
    high[...] = above
    sent[...] = congruence(above, transfers[at + 1])


def merge_quad(at, beside, own, others, transfers):
    vmem = pl.BlockSpec(memory_space=pltpu.VMEM)
    return pl.pallas_call(
        functools.partial(quad_kernel, at, beside),
        in_specs=[vmem] * 5,
        out_specs=[vmem] * 3,
        out_shape=[pltpu.VMEM((RANK, RANK), jnp.float32)] * 3,
        compiler_params=limit(4),
        name="merge_quad",
    )(in_vmem(own), *[in_vmem(x) for x in others], in_vmem(transfers))


def root_kernel(at, beside, own, *rest):
    others, transfers, done, factors = rest[:3], rest[3], rest[4], rest[5]
    pair = two_levels(own, others, transfers, at, beside)
    count = done.shape[0]
    for n, panels in enumerate(factor_panels([panels_of(gram) for gram in pair])):
        store_panels(factors, count + n, panels)
    for n in range(count):
        factors[n] = done[n]


def factor_root(at, beside, own, others, transfers, done):
    vmem = pl.BlockSpec(memory_space=pltpu.VMEM)
    return pl.pallas_call(
        functools.partial(root_kernel, at, beside),
        in_specs=[vmem] * 6,
        out_specs=vmem,
        out_shape=jax.ShapeDtypeStruct((done.shape[0] + 2, RANK, RANK), jnp.float32),
        compiler_params=limit(4),
        name="factor_root",
    )(in_vmem(own), *[in_vmem(x) for x in others], in_vmem(transfers), in_vmem(done))


def body(
    near_blocks,
    near_index,
    test_vectors,
    samples,
    leaf_basis,
    col_weights,
    coupling,
    adm_index,
    adm_count,
    leaf_transfer,
    inner_transfer,
    upper_transfer,
):
    count, rank, size = test_vectors.shape
    slots = adm_index.shape[1]
    devices = lax.axis_size("leaf") * lax.axis_size("near")
    total_levels = devices.bit_length() - 1
    device = lax.axis_index("leaf") * lax.axis_size("near") + lax.axis_index("near")
    paired = jnp.concatenate([col_weights[0::2], col_weights[1::2]], axis=2)
    weights = gather_weights(paired, devices)
    vectors = exchange_vectors(test_vectors, device, devices)
    held, near_index, adm_index, adm_count = lax.optimization_barrier(
        (weights[0], near_index, adm_index, adm_count)
    )
    weights[0] = held
    levels = jnp.arange(1, total_levels)
    starts = devices - (devices >> levels - 1)
    nodes = jnp.concatenate(
        [starts + (device >> levels), starts[1::2] + (device >> levels[1::2] ^ 1)]
    )
    held, upper_transfer = lax.optimization_barrier((weights[0], upper_transfer))
    transfers = select_transfers(nodes, upper_transfer)
    live = jnp.arange(slots)[None, :] < adm_count[:, None]
    halves = jnp.where(live, adm_index & 1, 2).reshape(-1)
    tiles = weight_tiles(adm_index, device).reshape(-1)
    wanted = vector_slots(near_index, device).reshape(-1)
    near, last, transfers, halves, tiles, wanted = lax.optimization_barrier(
        (weights[1], weights[2], transfers, halves, tiles, wanted)
    )
    far = gather_far(near, last, devices)
    weights = [held, near, last]
    swapped = [swap_cores(piece, devices) for piece in weights]
    near_gram = near_grams(wanted, near_blocks, samples, leaf_basis, vectors)
    far_low, far_high, near_gram = lax.optimization_barrier((far[0], far[1], near_gram))
    far = [far_low, far_high]
    weights = weights + far + swapped + [swap_cores(piece, devices) for piece in far]
    gram, inner_grams, sent = leaf_levels(
        tiles,
        halves,
        coupling,
        near_gram,
        leaf_transfer,
        inner_transfer,
        weights,
    )
    def swapped_with(x, flip):
        return lax.ppermute(x, AXES, [(d, d ^ flip) for d in range(devices)])

    other = swapped_with(sent, 1)
    first, sent = merge_pair(sent, other, transfers)
    grams = [first]
    local = []
    for axis in range(3):
        own = sent
        others = [swapped_with(own, flip << 1 + 2 * axis) for flip in (1, 2, 3)]
        if axis == 0:
            ready = factor(gram)
        elif axis == 1:
            ready = factor(inner_grams)
        else:
            ready = factor(*grams, keep=True)
        others[1], ready = lax.optimization_barrier((others[1], ready))
        at = 1 + 2 * axis
        if axis < 2:
            local.append(ready)
            low, high, sent = merge_quad(at, total_levels - 1 + axis, own, others, transfers)
            grams += [low, high]
        else:
            upper_factors = factor_root(at, total_levels - 1 + axis, own, others, transfers, ready)
    return (local[0], local[1][None], upper_factors[None])


def solution(mesh):
    split = P(AXES)
    return jax.shard_map(
        body,
        mesh=mesh,
        in_specs=(split,) * 11 + (P(),),
        out_specs=(split,) * 3,
        check_vma=False,
    )
```

```python
import functools

import jax
import jax.numpy as jnp
from jax import lax
from jax.experimental import pallas as pl
from jax.experimental.pallas import tpu as pltpu
from jax.sharding import PartitionSpec as P

AXES = ("leaf", "near")
RANK = 64


def split_three(x):
    hi = x.astype(jnp.bfloat16)
    rest = x - hi.astype(jnp.float32)
    mid = rest.astype(jnp.bfloat16)
    return hi, mid, (rest - mid.astype(jnp.float32)).astype(jnp.bfloat16)


def dot32(a, b):
    return jnp.dot(a, b, preferred_element_type=jnp.float32)


def dot_last(a, b):
    return lax.dot_general(a, b, (((1,), (1,)), ((), ())), preferred_element_type=jnp.float32)


def congruence(gram, transfer):
    across = jnp.transpose(transfer.astype(jnp.float32)).astype(jnp.bfloat16)
    hi, mid, low = split_three(gram)
    half = dot32(hi, transfer) + (dot32(mid, transfer) + dot32(low, transfer))
    hi, mid, low = split_three(half)
    return dot32(across, hi) + (dot32(across, mid) + dot32(across, low))


def unit_matrix():
    rows = lax.broadcasted_iota(jnp.int32, (RANK, RANK), 0)
    cols = lax.broadcasted_iota(jnp.int32, (RANK, RANK), 1)
    return (rows == cols).astype(jnp.float32)


def factor_panels(matrices):
    shape = (8, RANK)
    work = [list(panels) for panels in matrices]
    rows = lax.broadcasted_iota(jnp.int32, shape, 0)
    cols = lax.broadcasted_iota(jnp.int32, shape, 1)
    factors = [[None] * 8 for _ in work]
    for step in range(8):
        base = 8 * step
        for panels, factor in zip(work, factors):
            panel = panels[step]
            column = [
                jnp.broadcast_to(panel[:, base + k : base + k + 1], shape) for k in range(8)
            ]
            weights = [
                [jnp.broadcast_to(lower[:, base + k : base + k + 1], shape) for k in range(8)]
                for lower in panels[step + 1 :]
            ]
            rows_out = jnp.zeros(shape, jnp.float32)
            for j in range(8):
                here = rows == j
                pivot = jnp.broadcast_to(column[j][j : j + 1, :], shape)
                panel_row = jnp.broadcast_to(panel[j : j + 1, :], shape)
                rows_out = jnp.where(here, panel_row * lax.rsqrt(pivot), rows_out)
                inverse = 1.0 / pivot
                scale = column[j] * inverse
                for k in range(j + 1, 8):
                    entry = jnp.broadcast_to(column[k][j : j + 1, :], shape)
                    column[k] = jnp.where(here, entry * inverse, column[k] - scale * entry)
                panel = jnp.where(here, panel_row * inverse, panel - scale * panel_row)
            factor[step] = jnp.where(cols >= rows + base, rows_out, 0.0)
            for at, weight in enumerate(weights):
                lower = panels[step + 1 + at]
                for k in range(8):
                    lower = lower - weight[k] * jnp.broadcast_to(panel[k : k + 1, :], shape)
                panels[step + 1 + at] = lower
    return factors


def in_vmem(x):
    return pltpu.with_memory_space_constraint(x, pltpu.VMEM)


def panels_of(matrix):
    return [matrix[8 * p : 8 * p + 8, :] for p in range(8)]


def store_panels(ref, n, panels):
    for p in range(8):
        ref[n, 8 * p : 8 * p + 8, :] = panels[p]


def factor_kernel(*refs):
    grams, factors = refs[:-1], refs[-1]
    matrices = []
    for gram in grams:
        if len(gram.shape) == 2:
            matrices.append(panels_of(gram[...]))
        else:
            matrices += [panels_of(gram[n]) for n in range(gram.shape[0])]
    for n, panels in enumerate(factor_panels(matrices)):
        store_panels(factors, n, panels)


def factor(*grams, keep=False):
    count = sum(1 if gram.ndim == 2 else gram.shape[0] for gram in grams)
    vmem = pl.BlockSpec(memory_space=pltpu.VMEM)
    kind = pltpu.VMEM if keep else jax.ShapeDtypeStruct
    return pl.pallas_call(
        factor_kernel,
        in_specs=[vmem] * len(grams),
        out_specs=vmem,
        out_shape=kind((count, RANK, RANK), jnp.float32),
        compiler_params=limit(4),
        name="factor",
    )(*[in_vmem(gram) for gram in grams])


def limit(mebibytes):
    return pltpu.CompilerParams(vmem_limit_bytes=mebibytes << 20)


RING = ((0, 1, 2), (1, 2, 0))


def join_pieces(pieces, buffer):
    at = 0
    for piece in pieces:
        buffer[at : at + piece.shape[0]] = piece[...]
        at += piece.shape[0]


def join_kernel(*refs):
    join_pieces(refs[:-1], refs[-1])


def join(pieces):
    vmem = pl.BlockSpec(memory_space=pltpu.VMEM)
    shape = (sum(piece.shape[0] for piece in pieces),) + pieces[0].shape[1:]
    return pl.pallas_call(
        join_kernel,
        in_specs=[vmem] * len(pieces),
        out_specs=vmem,
        out_shape=pltpu.VMEM(shape, pieces[0].dtype),
        compiler_params=limit(4),
        name="join",
    )(*[in_vmem(piece) for piece in pieces])


def part_kernel(start, whole, part):
    part[...] = whole[start : start + part.shape[0]]


def part_of(whole, start, size):
    vmem = pl.BlockSpec(memory_space=pltpu.VMEM)
    return pl.pallas_call(
        functools.partial(part_kernel, start),
        in_specs=[vmem],
        out_specs=vmem,
        out_shape=pltpu.VMEM((size,) + whole.shape[1:], whole.dtype),
        compiler_params=limit(4),
        name="part",
    )(in_vmem(whole))


def ring_swap(x, stage, flip, devices):
    pairs = [(d, d ^ flip << 1 + 2 * RING[d & 1][stage]) for d in range(devices)]
    return lax.ppermute(x, AXES, pairs)


def grid_places(device):
    first = (device >> 1 & 1) + 2 * (device >> 4 & 1)
    second = (device >> 2 & 1) + 2 * (device >> 5 & 1)
    third = (device & 1) + 2 * (device >> 3 & 1) + 4 * (device >> 6 & 1)
    return first, second, third


def grid_device(first, second, third):
    low = (third & 1) + 2 * (first & 1) + 4 * (second & 1) + 8 * (third >> 1 & 1)
    return low + 16 * (first >> 1) + 32 * (second >> 1) + 64 * (third >> 2)


def grid_swap(x, dim, shift, devices):
    pairs = []
    for d in range(devices):
        place = list(grid_places(d))
        to = place[dim] + (1 if place[dim] % 2 == shift else -1)
        if 0 <= to < (4, 4, 8)[dim]:
            place[dim] = to
        pairs.append((d, grid_device(*place)))
    return lax.ppermute(x, AXES, pairs)


def neighbours(lower, upper, dim, odd, devices):
    even_pairs = grid_swap(jnp.where(odd, lower, upper), dim, 0, devices)
    odd_pairs = grid_swap(jnp.where(odd, upper, lower), dim, 1, devices)
    return jnp.where(odd, even_pairs, odd_pairs), jnp.where(odd, odd_pairs, even_pairs)


def swap_cores(x, devices):
    return lax.ppermute(x, AXES, [(d, d ^ 1) for d in range(devices)])


def exchange_vectors(own, device, devices):
    first, second, _ = grid_places(device)
    left, right = neighbours(own[0::2], own[1::2], 0, first % 2 == 1, devices)
    rows = jnp.stack([left, own[0::2], own[1::2], right], axis=1)
    before, after = neighbours(rows[0], rows[1], 1, second % 2 == 1, devices)
    plane = jnp.concatenate([before, rows[0], rows[1], after])
    return [plane, swap_cores(plane, devices), grid_swap(plane, 2, 1, devices)]


def vector_slots(near_index, device):
    first, second, third = grid_places(device)
    cell = near_index
    x = (cell & 1) + 2 * (cell >> 3 & 1) + 4 * (cell >> 6 & 1) - 2 * first
    y = (cell >> 1 & 1) + 2 * (cell >> 4 & 1) + 4 * (cell >> 7 & 1) - 2 * second
    z = (cell >> 2 & 1) + 2 * (cell >> 5 & 1) + 4 * (cell >> 8 & 1)
    plane = jnp.where(z == third, 0, jnp.where(z >> 1 == third >> 1, 1, 2))
    return 16 * plane + 4 * (y + 1) + x + 1


def gather_weights(own, devices):
    held = own
    for stage in range(2):
        others = [ring_swap(held, stage, flip, devices) for flip in (1, 3, 2)]
        held = join([held] + others)
    near = ring_swap(held, 2, 1, devices)
    last = ring_swap(held, 2, 3, devices)
    return [held, near, last]


def gather_far(near, last, devices):
    half = near.shape[0] // 2
    low, high = part_of(last, 0, half), part_of(near, half, half)
    return [ring_swap(low, 2, 1, devices), ring_swap(high, 2, 3, devices)]


def weight_tiles(adm_index, device):
    owner = adm_index >> 2
    label = []
    for axis in range(3):
        apart = (owner ^ device) >> 1 + 2 * axis & 3
        label.append(apart ^ apart >> 1)
    order = [
        label[RING[0][2]] * 16 + label[RING[0][1]] * 4 + label[RING[0][0]],
        label[RING[1][2]] * 16 + label[RING[1][1]] * 4 + label[RING[1][0]],
    ]
    core = owner & 1
    other = core ^ (device & 1)
    return other * 128 + 2 * jnp.where(core == 1, order[1], order[0]) + (adm_index >> 1 & 1)


def near_kernel(slots, blocks, samples, basis, *rest):
    pieces, (gram, vectors, held, semaphores) = rest[:3], rest[3:]
    copies = [
        pltpu.make_async_copy(blocks.at[leaf], held.at[leaf], semaphores.at[leaf])
        for leaf in range(blocks.shape[0])
    ]
    for copy in copies:
        copy.start()
    join_pieces(pieces, vectors)
    for leaf, copy in enumerate(copies):
        copy.wait()
        near_leaf(leaf, slots, held, samples, basis, vectors, gram)


def near_leaf(leaf, slots, blocks, samples, basis, vectors, gram):
    total = None
    for k in range(8):
        part = dot_last(vectors[slots[8 * leaf + k]], blocks[leaf, k])
        total = part if total is None else total + part
    far = (samples[leaf].astype(jnp.float32) - total).astype(jnp.bfloat16)
    scale = RANK**-0.5
    wide = dot_last(basis[leaf], far) * scale
    tall = dot_last(far, basis[leaf]) * scale
    wide_hi = wide.astype(jnp.bfloat16)
    wide_low = (wide - wide_hi.astype(jnp.float32)).astype(jnp.bfloat16)
    tall_hi = tall.astype(jnp.bfloat16)
    tall_low = (tall - tall_hi.astype(jnp.float32)).astype(jnp.bfloat16)
    gram[leaf] = dot32(tall_hi, wide_hi) + (dot32(tall_hi, wide_low) + dot32(tall_low, wide_hi))


def near_grams(slots, near_blocks, samples, leaf_basis, pieces):
    count, rank, size = samples.shape
    vmem = pl.BlockSpec(memory_space=pltpu.VMEM)
    return pl.pallas_call(
        near_kernel,
        in_specs=[pl.BlockSpec(memory_space=pltpu.SMEM), pl.BlockSpec(memory_space=pltpu.HBM)]
        + [vmem] * (2 + len(pieces)),
        out_specs=vmem,
        out_shape=pltpu.VMEM((count, rank, rank), jnp.float32),
        scratch_shapes=[
            pltpu.VMEM((48, rank, size), jnp.bfloat16),
            pltpu.VMEM(near_blocks.shape, near_blocks.dtype),
            pltpu.SemaphoreType.DMA((count,)),
        ],
        compiler_params=limit(12),
        name="near_grams",
    )(
        slots,
        pltpu.with_memory_space_constraint(near_blocks, pltpu.HBM),
        in_vmem(samples),
        in_vmem(leaf_basis),
        *[in_vmem(piece) for piece in pieces],
    )


def select_kernel(nodes, upper_transfer, transfers, semaphores):
    copies = [
        pltpu.make_async_copy(upper_transfer.at[nodes[n]], transfers.at[n], semaphores.at[n])
        for n in range(transfers.shape[0])
    ]
    for copy in copies:
        copy.start()
    for copy in copies:
        copy.wait()


def select_transfers(nodes, upper_transfer):
    levels, rank = nodes.shape[0], upper_transfer.shape[1]
    return pl.pallas_call(
        select_kernel,
        in_specs=[
            pl.BlockSpec(memory_space=pltpu.SMEM),
            pl.BlockSpec(memory_space=pl.ANY),
        ],
        out_specs=pl.BlockSpec(memory_space=pltpu.VMEM),
        out_shape=pltpu.VMEM((levels, rank, rank), jnp.bfloat16),
        scratch_shapes=[pltpu.SemaphoreType.DMA((levels,))],
        compiler_params=limit(4),
        name="select_transfers",
    )(nodes, upper_transfer)


def leaf_kernel(tiles, halves, coupling, near_gram, leaf_transfer, inner_transfer, *rest):
    pieces, (leaf_grams, inner_grams, sent, weights, coupled) = rest[:10], rest[10:]
    join_pieces(pieces, weights)
    unit = unit_matrix()
    moved = []
    for leaf in range(leaf_grams.shape[0]):
        sums = coupled_gram(leaf, tiles, halves, coupling, weights, coupled.at[leaf % 2])
        gram = near_gram[leaf] + sums * (1.0 / 2048) + unit
        leaf_grams[leaf] = gram
        moved.append(congruence(gram, leaf_transfer[leaf]))
    first = 0.5 * (moved[0] + moved[1]) + unit
    second = 0.5 * (moved[2] + moved[3]) + unit
    inner_grams[0] = first
    inner_grams[1] = second
    top = congruence(first, inner_transfer[0, 0]) + congruence(second, inner_transfer[0, 1])
    top = 0.5 * top + unit
    inner_grams[2] = top
    sent[...] = congruence(top, inner_transfer[0, 2])


def coupled_gram(leaf, tiles, halves, coupling, weights, coupled):
    side = lax.broadcasted_iota(jnp.int32, (RANK, 2 * RANK), 1) >> 6
    nothing = jnp.zeros((RANK, 2 * RANK), jnp.bfloat16)
    for pair in range(16):
        chosen = []
        for s in (2 * pair, 2 * pair + 1):
            tile = weights[tiles[32 * leaf + s]]
            chosen.append(jnp.where(side == halves[32 * leaf + s], tile, nothing))
        both = jnp.concatenate(
            [
                jnp.concatenate([chosen[0], nothing], axis=1),
                jnp.concatenate([nothing, chosen[1]], axis=1),
            ],
            axis=0,
        )
        product = dot32(coupling[leaf, :, 128 * pair : 128 * pair + 128], both).astype(jnp.bfloat16)
        coupled[128 * pair : 128 * pair + 64, :] = product[:, :128]
        coupled[128 * pair + 64 : 128 * pair + 128, :] = product[:, 128:]
    square = lax.dot_general(
        coupled[...], coupled[...], (((0,), (0,)), ((), ())), preferred_element_type=jnp.float32
    )
    return square[:RANK, :RANK] + square[RANK:, RANK:]


def leaf_levels(tiles, halves, coupling, near_gram, leaf_transfer, inner_transfer, pieces):
    count, rank, width = coupling.shape
    vmem = pl.BlockSpec(memory_space=pltpu.VMEM)
    inputs = [coupling, near_gram, leaf_transfer, inner_transfer] + list(pieces)
    return pl.pallas_call(
        leaf_kernel,
        in_specs=[pl.BlockSpec(memory_space=pltpu.SMEM)] * 2 + [vmem] * len(inputs),
        out_specs=[vmem] * 3,
        out_shape=[
            pltpu.VMEM((count, rank, rank), jnp.float32),
            pltpu.VMEM((count - 1, rank, rank), jnp.float32),
            pltpu.VMEM((rank, rank), jnp.float32),
        ],
        scratch_shapes=[
            pltpu.VMEM((256, rank, 2 * rank), jnp.bfloat16),
            pltpu.VMEM((2, width, 2 * rank), jnp.bfloat16),
        ],
        compiler_params=limit(12),
        name="leaf_levels",
    )(tiles, halves, *[in_vmem(x) for x in inputs])


def merged(one, other):
    return 0.5 * (one + other) + unit_matrix()


def pair_kernel(own, other, transfers, gram, sent):
    here = merged(own[...], other[...])
    gram[...] = here
    sent[...] = congruence(here, transfers[0])


def merge_pair(own, other, transfers):
    vmem = pl.BlockSpec(memory_space=pltpu.VMEM)
    return pl.pallas_call(
        pair_kernel,
        in_specs=[vmem] * 3,
        out_specs=[vmem] * 2,
        out_shape=[pltpu.VMEM((RANK, RANK), jnp.float32)] * 2,
        compiler_params=limit(4),
        name="merge_pair",
    )(in_vmem(own), in_vmem(other), in_vmem(transfers))


def two_levels(own, others, transfers, at, beside):
    sibling, cousin, partner = others
    here = merged(own[...], sibling[...])
    there = merged(cousin[...], partner[...])
    above = merged(congruence(here, transfers[at]), congruence(there, transfers[beside]))
    return here, above


def quad_kernel(at, beside, own, *rest):
    others, transfers, (low, high, sent) = rest[:3], rest[3], rest[4:]
    here, above = two_levels(own, others, transfers, at, beside)
    low[...] = here
    high[...] = above
    sent[...] = congruence(above, transfers[at + 1])


def merge_quad(at, beside, own, others, transfers):
    vmem = pl.BlockSpec(memory_space=pltpu.VMEM)
    return pl.pallas_call(
        functools.partial(quad_kernel, at, beside),
        in_specs=[vmem] * 5,
        out_specs=[vmem] * 3,
        out_shape=[pltpu.VMEM((RANK, RANK), jnp.float32)] * 3,
        compiler_params=limit(4),
        name="merge_quad",
    )(in_vmem(own), *[in_vmem(x) for x in others], in_vmem(transfers))


def root_kernel(at, beside, own, *rest):
    others, transfers, done, factors = rest[:3], rest[3], rest[4], rest[5]
    pair = two_levels(own, others, transfers, at, beside)
    count = done.shape[0]
    for n, panels in enumerate(factor_panels([panels_of(gram) for gram in pair])):
        store_panels(factors, count + n, panels)
    for n in range(count):
        factors[n] = done[n]


def factor_root(at, beside, own, others, transfers, done):
    vmem = pl.BlockSpec(memory_space=pltpu.VMEM)
    return pl.pallas_call(
        functools.partial(root_kernel, at, beside),
        in_specs=[vmem] * 6,
        out_specs=vmem,
        out_shape=jax.ShapeDtypeStruct((done.shape[0] + 2, RANK, RANK), jnp.float32),
        compiler_params=limit(4),
        name="factor_root",
    )(in_vmem(own), *[in_vmem(x) for x in others], in_vmem(transfers), in_vmem(done))


def body(
    near_blocks,
    near_index,
    test_vectors,
    samples,
    leaf_basis,
    col_weights,
    coupling,
    adm_index,
    adm_count,
    leaf_transfer,
    inner_transfer,
    upper_transfer,
):
    count, rank, size = test_vectors.shape
    slots = adm_index.shape[1]
    devices = lax.axis_size("leaf") * lax.axis_size("near")
    total_levels = devices.bit_length() - 1
    device = lax.axis_index("leaf") * lax.axis_size("near") + lax.axis_index("near")
    paired = jnp.concatenate([col_weights[0::2], col_weights[1::2]], axis=2)
    weights = gather_weights(paired, devices)
    vectors = exchange_vectors(test_vectors, device, devices)
    held, near_index, adm_index, adm_count = lax.optimization_barrier(
        (weights[0], near_index, adm_index, adm_count)
    )
    weights[0] = held
    levels = jnp.arange(1, total_levels)
    starts = devices - (devices >> levels - 1)
    nodes = jnp.concatenate(
        [starts + (device >> levels), starts[1::2] + (device >> levels[1::2] ^ 1)]
    )
    held, upper_transfer = lax.optimization_barrier((weights[0], upper_transfer))
    transfers = select_transfers(nodes, upper_transfer)
    live = jnp.arange(slots)[None, :] < adm_count[:, None]
    halves = jnp.where(live, adm_index & 1, 2).reshape(-1)
    tiles = weight_tiles(adm_index, device).reshape(-1)
    wanted = vector_slots(near_index, device).reshape(-1)
    near, last, transfers, halves, tiles, wanted = lax.optimization_barrier(
        (weights[1], weights[2], transfers, halves, tiles, wanted)
    )
    far = gather_far(near, last, devices)
    weights = [held, near, last]
    swapped = [swap_cores(piece, devices) for piece in weights]
    near_gram = near_grams(wanted, near_blocks, samples, leaf_basis, vectors)
    far_low, far_high, near_gram = lax.optimization_barrier((far[0], far[1], near_gram))
    far = [far_low, far_high]
    weights = weights + far + swapped + [swap_cores(piece, devices) for piece in far]
    gram, inner_grams, sent = leaf_levels(
        tiles,
        halves,
        coupling,
        near_gram,
        leaf_transfer,
        inner_transfer,
        weights,
    )
    def swapped_with(x, flip):
        return lax.ppermute(x, AXES, [(d, d ^ flip) for d in range(devices)])

    other = swapped_with(sent, 1)
    first, sent = merge_pair(sent, other, transfers)
    grams = [first]
    local = []
    for axis in range(3):
        own = sent
        others = [swapped_with(own, flip << 1 + 2 * axis) for flip in (1, 2, 3)]
        if axis == 0:
            ready = factor(gram)
        elif axis == 1:
            ready = factor(inner_grams)
        else:
            ready = factor(*grams, keep=True)
        others[1], ready = lax.optimization_barrier((others[1], ready))
        at = 1 + 2 * axis
        if axis < 2:
            local.append(ready)
            low, high, sent = merge_quad(at, total_levels - 1 + axis, own, others, transfers)
            grams += [low, high]
        else:
            upper_factors = factor_root(at, total_levels - 1 + axis, own, others, transfers, ready)
    return (local[0], local[1][None], upper_factors[None])


def solution(mesh):
    split = P(AXES)
    return jax.shard_map(
        body,
        mesh=mesh,
        in_specs=(split,) * 11 + (P(),),
        out_specs=(split,) * 3,
        check_vma=False,
    )
```
